1024 devices in a mesh: gx: 32 (over z), gy: 8 (over x, core), gz: 4 (over y).
Axes of the slice: x: 4, y: 4, z: 32, core: 2. Of those that a mesh axis runs over, the one named last changes fastest.
Arguments:
- pops: float32 [19, 32, 64, 4096], P(None, 'gz', 'gy', 'gx'), may hold values from 0.4 to 1.6
- coarse_pops: bfloat16 [19, 32, 64, 4096], P(None, 'gz', 'gy', 'gx'), may hold values from 0.3984375 to 1.59375
- interface: int32 [32, 64, 4096], P('gz', 'gy', 'gx'), may hold values 0 or 1
- drop_vel: float32 [3, 16384, 128], P(None, ('gx', 'gy', 'gz')), may hold values from -1 to 1
- drop_frac: float32 [3, 16384, 128], P(None, ('gx', 'gy', 'gz')), may hold values from 0 to 1
- home: int32 [16384, 128], P(('gx', 'gy', 'gz')), may hold values from 0 to 8191, as said below
- counts: int32 [16384], P(('gx', 'gy', 'gz')), may hold values from 1 to 128, 1572864 in all
- dest: int32 [16384], P(('gx', 'gy', 'gz')), may hold values from 0 to 26, as said below
Outputs:
- pops_out: float32 [19, 32, 64, 4096], P(None, 'gz', 'gy', 'gx')
- force: float32 [3, 32, 64, 4096], P(None, 'gz', 'gy', 'gx')
- arrived: float32 [6, 69632, 128], P(None, ('gx', 'gy', 'gz'))
The draws below stay inside these ranges and needn't reach their ends.
Inputs may be any that keep to these rules, and one draw needn't show every extreme that they name: All droplets of a block lie in one tile of 8 x 8 x 8 cells at tile-aligned offsets; home = (8 * z + y) * 128 + x in the device's brick. `counts`: live droplets fill the first slots of their block. `dest`: no block crosses a wall along z; apart from code 13, at most 2 blocks of one device share a code, and every device has exactly 2 blocks of some code other than 13.
All inputs are finite; a program needn't handle non-finite values. No bound on the sum of `interface` on one device may be relied on, other than what follows from the above.
Results may differ from the reference program's by a relative error of at most 0.0003.
Values sent between devices are 32-bit elements; how exact they have to be, the bound alone decides.
A program may use at most 32 MiB of HBM per device.

```python
import math
import jax
import jax.numpy as jnp
import numpy as np
from jax import lax

CX = 128
CY = 8
CZ = 8
NBD = 16
TILE = 8
CAP = 2
NX = 4096
NY = 64
NZ = 32
NBT = 16384
SLOTS = 68
N_GX = 32
N_GY = 8
N_GZ = 4
DEVICES = 1024


def draw_home(key, part):
    tiles_x = CX // TILE
    tiles_y = CY // TILE
    tiles_z = CZ // TILE
    key_tile, key_x, key_y, key_z = jax.random.split(key, 4)
    tile = jax.random.randint(key_tile, (NBT, 1), 0, tiles_x * tiles_y * tiles_z)
    tile_x = tile % tiles_x
    tile_y = tile // tiles_x % tiles_y
    tile_z = tile // (tiles_x * tiles_y)
    cell_x = tile_x * TILE + jax.random.randint(key_x, (NBT, 128), 0, TILE)
    cell_y = tile_y * TILE + jax.random.randint(key_y, (NBT, 128), 0, TILE)
    cell_z = tile_z * TILE + jax.random.randint(key_z, (NBT, 128), 0, TILE)
    return ((cell_z * CY + cell_y) * CX + cell_x).astype(jnp.int32)


def draw_dest(key, part):
    plane_codes = jnp.array([9, 10, 11, 12, 14, 15, 16, 17], dtype=jnp.int32)
    travel = jnp.concatenate([jnp.arange(13, dtype=jnp.int32), jnp.arange(14, 27, dtype=jnp.int32)])
    pool = jnp.concatenate([jnp.repeat(travel, CAP), jnp.full((NBD,), 13, dtype=jnp.int32)])

    def one_device(index):
        device_key = jax.random.fold_in(jax.random.fold_in(key, 7321), index)
        key_pick, key_pool, key_order = jax.random.split(device_key, 3)
        level = index % N_GZ
        chosen = plane_codes[jax.random.randint(key_pick, (), 0, 8)]
        options = jnp.where(pool == chosen, 13, pool)
        picked = options[jax.random.permutation(key_pool, options.shape[0])[:NBD - CAP]]
        codes = jnp.concatenate([jnp.full((CAP,), chosen, dtype=jnp.int32), picked])
        codes = codes[jax.random.permutation(key_order, NBD)]
        travel_z = codes // 9 - 1
        blocked = (level == 0) & (travel_z == -1) | (level == N_GZ - 1) & (travel_z == 1)
        return jnp.where(blocked, 13, codes).astype(jnp.int32)
    return jax.vmap(one_device)(jnp.arange(DEVICES, dtype=jnp.int32)).reshape(NBT)


def with_ends(result, rng, smallest, high):
    longest = result.shape.index(max(result.shape))
    spots = []
    for shift in (0, 1):
        where = [jax.random.randint(jax.random.fold_in(rng, axis), (), 0, length) for axis, length in enumerate(result.shape)]
        where[longest] = (where[longest] + shift) % result.shape[longest]
        spots.append(tuple(where))
    return result.at[spots[0]].set(smallest).at[spots[1]].set(high)


def block_scale(own_key, dims, shards, smallest, largest):
    def one(axis_at, parts):
        steps = jax.random.uniform(jax.random.fold_in(jax.random.fold_in(own_key, 6), axis_at), (parts,), jnp.float32, smallest / len(shards), largest / len(shards))
        return jnp.repeat(jnp.exp(steps), dims[axis_at] // parts).reshape((-1,) + (1,) * (len(dims) - axis_at - 1))

    level = one(*shards[0])
    for cut in shards[1:]:
        level = level * one(*cut)
    return level


def profile(count, total, bound, skew):
    portions = [(1 << 20) // math.isqrt(grade ** skew) + 1 for grade in range(2, count + 1)]
    surplus, holding = total - bound - (count - 1), [1] * (count - 1)
    while surplus > 0:
        free = [i for i in range(count - 1) if holding[i] < bound]
        whole, remaining = sum([portions[i] for i in free]), surplus
        for i in free:
            addition = min(bound - holding[i], max(1, remaining * portions[i] // whole), surplus)
            holding[i] = holding[i] + addition
            surplus = surplus - addition
    return np.array([bound] + holding)


def ragged(key, number_of, total, bound, slope):
    if number_of == 2:
        one = jax.random.randint(key, (), max(1, total - bound), min(bound, total - 1) + 1)
        return jnp.stack([one, total - one])
    lengths = jnp.asarray(profile(number_of, total, bound, slope), jnp.int32)
    couples = (number_of - 1) // 2
    giver, taker = lengths[1:1 + 2 * couples:2], lengths[2:2 + 2 * couples:2]
    margin = jnp.minimum(giver - 1, bound - taker)
    moved = jax.random.randint(jax.random.fold_in(key, 1), (couples,), 0, 1 << 20) % (margin + 1)
    lengths = lengths.at[1:1 + 2 * couples:2].set(giver - moved).at[2:2 + 2 * couples:2].set(taker + moved)
    return lengths[jax.random.permutation(jax.random.fold_in(key, 2), number_of)]


def scatter_about(key, dims, width, reach, cuts=(), kind=jnp.bfloat16):
    loudness = block_scale(key, dims, cuts, -0.22, 0.18) if cuts else 1.0
    values = jax.random.normal(key, dims, jnp.float32) * width * loudness
    return jnp.minimum(jnp.maximum(values, -reach), reach).astype(kind)


def setup_inputs(seed: int = 0) -> dict:
    key_of = jax.random.split(jax.random.key(seed), 9)
    pops = jnp.clip(0.4 + 1.2 * jax.random.uniform(key_of[0], (19, NZ, NY, NX), jnp.float32) ** block_scale(key_of[0], (19, NZ, NY, NX), ((1, 4), (2, 8), (3, 32)), -0.2, 0.2), 0.4, 1.6)
    coarse_pops = jnp.clip(0.3984375 + 1.1953125 * jax.random.uniform(key_of[1], (19, NZ, NY, NX), jnp.float32) ** block_scale(key_of[1], (19, NZ, NY, NX), ((1, 4), (2, 8), (3, 32)), -0.2, 0.2), 0.3984375, 1.59375).astype(jnp.bfloat16)
    interface = with_ends((jax.random.randint(key_of[2], (NZ, NY, NX), 0, 4) < 1).astype(jnp.int32), jax.random.fold_in(key_of[2], 1), 0, 1)
    drop_vel = scatter_about(key_of[3], (3, NBT, 128), 0.2, 1.0, ((1, 1024),), jnp.float32)
    drop_frac = jnp.clip(1.0 * jax.random.uniform(key_of[4], (3, NBT, 128), jnp.float32) ** block_scale(key_of[4], (3, NBT, 128), ((1, 1024),), -0.2, 0.2), 0.0, 1.0)
    home = draw_home(jax.random.fold_in(key_of[8], 71), 0)
    counts = ragged(key_of[6], NBT, NBT * 96, 128, 1).astype(jnp.int32)
    dest = draw_dest(jax.random.fold_in(key_of[8], 71), 0)
    return {"pops": pops, "coarse_pops": coarse_pops, "interface": interface, "drop_vel": drop_vel, "drop_frac": drop_frac, "home": home, "counts": counts, "dest": dest}


lattice = np.array([[0, 0, 0], [1, 0, 0], [-1, 0, 0], [0, 1, 0], [0, -1, 0], [0, 0, 1], [0, 0, -1],
                    [1, 1, 0], [-1, -1, 0], [1, -1, 0], [-1, 1, 0], [1, 0, 1], [-1, 0, -1], [1, 0, -1],
                    [-1, 0, 1], [0, 1, 1], [0, -1, -1], [0, 1, -1], [0, -1, 1]])
weights_table = np.array([1.0 / 3.0] + [1.0 / 18.0] * 6 + [1.0 / 36.0] * 12)
opposite = [0, 2, 1, 4, 3, 6, 5, 8, 7, 10, 9, 12, 11, 14, 13, 16, 15, 18, 17]
inverse_tau = 0.8
relax = 0.5
couple = 8.0


def kernel(distance):
    return 0.25 * (1.0 + jnp.cos(math.pi * 0.5 * distance))


def macroscopic(pops):
    density = pops[0] * float(weights_table[0])
    moment = [jnp.zeros_like(density), jnp.zeros_like(density), jnp.zeros_like(density)]
    for index in range(1, 19):
        term = pops[index] * float(weights_table[index])
        density = density + term
        for axis in range(3):
            if int(lattice[index][axis]) != 0:
                moment[axis] = moment[axis] + float(lattice[index][axis]) * term
    return density, [moment[axis] / density for axis in range(3)]


def collide(pops, coarse, interface):
    density, flow = macroscopic(pops)
    square = flow[0] * flow[0] + flow[1] * flow[1] + flow[2] * flow[2]
    inside = interface == 1
    posts = []
    for index in range(19):
        along = jnp.zeros_like(density)
        for axis in range(3):
            if int(lattice[index][axis]) != 0:
                along = along + float(lattice[index][axis]) * flow[axis]
        balance = density * (1.0 + 3.0 * along + 4.5 * along * along - 1.5 * square)
        relaxed = pops[index] - (pops[index] - balance) * inverse_tau
        posts.append(jnp.where(inside, coarse[index].astype(jnp.float32), relaxed))
    return jnp.stack(posts)


def stream(posts):
    pulled = []
    for index in range(19):
        move_x = int(lattice[index][0])
        move_y = int(lattice[index][1])
        move_z = int(lattice[index][2])
        moved = jnp.roll(posts[index], (move_z, move_y, move_x), axis=(0, 1, 2))
        back = posts[opposite[index]]
        if move_z == 1:
            moved = moved.at[0].set(back[0])
        if move_z == -1:
            moved = moved.at[-1].set(back[-1])
        pulled.append(moved)
    return jnp.stack(pulled)


def reference(pops, coarse_pops, interface, drop_vel, drop_frac, home, counts, dest):
    state = pops
    for substep in range(2):
        state = stream(collide(state, coarse_pops, interface))
    density, flow = macroscopic(state)
    cells_all = NZ * NY * NX
    flat_velocity = jnp.stack(flow).reshape(3, cells_all)

    device = jnp.arange(NBT, dtype=jnp.int32) // NBD
    pos_x = device // (N_GY * N_GZ)
    pos_y = (device // N_GZ) % N_GY
    pos_z = device % N_GZ
    cell_x = pos_x[:, None] * CX + home % CX
    cell_y = pos_y[:, None] * CY + (home // CX) % CY
    cell_z = pos_z[:, None] * CZ + home // (CX * CY)

    def stencil(offset):
        step_z = offset // 16
        step_y = (offset // 4) % 4
        step_x = offset % 4
        weight = kernel((step_z - 1) - drop_frac[2]) * kernel((step_y - 1) - drop_frac[1]) * kernel((step_x - 1) - drop_frac[0])
        layer = cell_z + step_z - 1
        inside = (layer >= 0) & (layer < NZ)
        flat = (jnp.clip(layer, 0, NZ - 1) * NY + (cell_y + step_y - 1) % NY) * NX + (cell_x + step_x - 1) % NX
        return weight, inside, flat.astype(jnp.int32)

    def gather_step(total, offset):
        weight, inside, flat = stencil(offset)
        sample = flat_velocity[:, flat]
        return total + jnp.where(inside, weight, 0.0) * sample, None

    offsets = jnp.arange(64, dtype=jnp.int32)
    sampled = lax.scan(gather_step, jnp.zeros((3, NBT, 128), jnp.float32), offsets)[0]
    moved = drop_vel + relax * (sampled - drop_vel)
    live = (jnp.arange(128, dtype=jnp.int32)[None, :] < counts[:, None])[None]
    push = jnp.where(live, couple * (moved - sampled), 0.0)

    def spread_step(total, offset):
        weight, inside, flat = stencil(offset)
        target = jnp.where(inside, flat, cells_all)
        return total.at[:, target].add(weight * push, mode="drop"), None

    force = lax.scan(spread_step, jnp.zeros((3, cells_all), jnp.float32), offsets)[0].reshape(3, NZ, NY, NX)

    states = jnp.where(live, jnp.concatenate([moved, drop_frac + moved], axis=0), 0.0)
    travel_x = dest % 3 - 1
    travel_y = (dest // 3) % 3 - 1
    travel_z = dest // 9 - 1
    target = (((pos_x + travel_x) % N_GX) * N_GY + (pos_y + travel_y) % N_GY) * N_GZ + (pos_z + travel_z) % N_GZ
    grouped = dest.reshape(DEVICES, NBD)
    order = jnp.arange(NBD, dtype=jnp.int32)
    earlier = (grouped[:, :, None] == grouped[:, None, :]) & (order[None, None, :] < order[None, :, None])
    rank = jnp.sum(earlier.astype(jnp.int32), axis=2).reshape(NBT)
    lane = jnp.where(dest < 13, dest, dest - 1)
    slot = jnp.where(dest == 13, device * SLOTS + jnp.arange(NBT, dtype=jnp.int32) % NBD,
                     target * SLOTS + NBD + lane * CAP + rank).astype(jnp.int32)
    arrived = jnp.zeros((6, DEVICES * SLOTS, 128), jnp.float32).at[:, slot].set(states)
    return state, force, arrived
```

```python
import math

import jax
import jax.numpy as jnp
import numpy as np
from jax import lax
from jax.experimental import pallas as pl
from jax.experimental.pallas import tpu as pltpu
from jax.sharding import PartitionSpec as P

lattice = [
    (0, 0, 0), (1, 0, 0), (-1, 0, 0), (0, 1, 0), (0, -1, 0), (0, 0, 1), (0, 0, -1),
    (1, 1, 0), (-1, -1, 0), (1, -1, 0), (-1, 1, 0), (1, 0, 1), (-1, 0, -1), (1, 0, -1),
    (-1, 0, 1), (0, 1, 1), (0, -1, -1), (0, 1, -1), (0, -1, 1),
]
weights_table = [1.0 / 3.0] + [1.0 / 18.0] * 6 + [1.0 / 36.0] * 12
opposite = [0, 2, 1, 4, 3, 6, 5, 8, 7, 10, 9, 12, 11, 14, 13, 16, 15, 18, 17]
inverse_tau = 0.8
relax = 0.5
couple = 8.0
f32 = jnp.float32
bf16 = jnp.bfloat16

face_pops = {}
for axis in range(3):
    for sign in (1, -1):
        d = [0, 0, 0]
        d[axis] = sign
        face_pops[tuple(d)] = [i for i in range(19) if lattice[i][axis] == sign]
post_msgs = {}
tiles = 0
for i in range(1, 19):
    c = lattice[i]
    count = 1 if (abs(c[0]) + abs(c[1]) + abs(c[2]) > 1 or c[0] != 0) else 5
    post_msgs[c] = (tiles, count)
    tiles += count
POST_TILES = tiles

regions = {
    (0, 0): (0, 24),
    (-1, 0): (24, 6),
    (1, 0): (30, 3),
    (0, -1): (33, 6),
    (0, 1): (39, 3),
    (-1, -1): (42, 2),
    (1, -1): (44, 1),
    (-1, 1): (45, 1),
    (1, 1): (46, 1),
}
region_list = list(regions)
ROWS = 48 * 8
all_dirs = [(x, y, z) for z in (-1, 0, 1) for y in (-1, 0, 1) for x in (-1, 0, 1) if (x, y, z) != (0, 0, 0)]
N_POST = 18
N_MSG = 2 * N_POST + 3 * 26
PAIRS = 8
BLOCKS = 16


def corner_rows(region):
    dy, dz = region
    ys = [7] if dy == 1 else [0, 1]
    zs = [7] if dz == 1 else [0, 1]
    return [(c, y, z) for c in range(3) for z in zs for y in ys]


def tile_rows(t):
    return pl.ds(t * 8, 8)


def kernel(
    sizes,
    pops, coarse, interface, drop_vel, drop_frac, home, counts, dest,
    state_hbm, force, arrived,
    posts, state, psend, precv, vmain, vhalo, vsend, pksend, pkrecv, vhi, vlo, whi, wlo,
    taps, homes, shi, slo, facc, fsend, frecv, fpsend, fprecv, states, outbox, inbox,
    send_sem, recv_sem, out_sem,
):
    n_x, n_y, n_z = sizes
    me = (lax.axis_index("gx"), lax.axis_index("gy"), lax.axis_index("gz"))
    level = me[2]
    at_bottom = level == 0
    at_top = level == n_z - 1

    def moved_by(axis, step, size):
        if step == 0:
            return me[axis]
        return lax.rem(me[axis] + (step + size), size)

    coords = {
        (axis, step): moved_by(axis, step, size)
        for axis, size in enumerate(sizes)
        for step in (-1, 0, 1)
    }

    def device(d):
        return {"gx": coords[0, d[0]], "gy": coords[1, d[1]], "gz": coords[2, d[2]]}

    lane = lax.broadcasted_iota(jnp.int32, (8, 128), 1)
    sub = lax.broadcasted_iota(jnp.int32, (8, 128), 0)

    started = []

    def copy(index, src, dst, d):
        made = pltpu.make_async_remote_copy(
            src_ref=src,
            dst_ref=dst,
            send_sem=send_sem.at[index],
            recv_sem=recv_sem.at[index],
            device_id=device(d),
            device_id_type=pl.DeviceIdType.MESH,
        )
        made.start()
        started.append(made)
        return made

    barrier = pltpu.get_barrier_semaphore()
    for d in all_dirs:
        pl.semaphore_signal(barrier, inc=1, device_id=device(d), device_id_type=pl.DeviceIdType.MESH)

    def macroscopic(values):
        density = values[0] * weights_table[0]
        moment = [None, None, None]
        for index in range(1, 19):
            term = values[index] * weights_table[index]
            density = density + term
            for axis in range(3):
                sign = lattice[index][axis]
                if sign == 1:
                    moment[axis] = term if moment[axis] is None else moment[axis] + term
                if sign == -1:
                    moment[axis] = moment[axis] - term
        inverse = 1.0 / density
        return density, [m * inverse for m in moment]

    def collide(source):
        @pl.loop(0, 8)
        def _(z):
            rows = pl.ds(pl.multiple_of(z * 8, 8), 8)
            values = [source[i, rows, :] for i in range(19)]
            density, flow = macroscopic(values)
            square = flow[0] * flow[0] + flow[1] * flow[1] + flow[2] * flow[2]
            inside = interface[z] == 1
            base = 1.0 - 1.5 * square
            for i in range(19):
                along = None
                for axis in range(3):
                    sign = lattice[i][axis]
                    if sign == 1:
                        along = flow[axis] if along is None else along + flow[axis]
                    if sign == -1:
                        along = -flow[axis] if along is None else along - flow[axis]
                if along is None:
                    balance = density * base
                else:
                    balance = density * (base + along * (3.0 + 4.5 * along))
                relaxed = values[i] - (values[i] - balance) * inverse_tau
                posts[i, rows, :] = jnp.where(inside, coarse[i, z].astype(f32), relaxed)

    def send_posts(r):
        copies = {}
        for number, (d, (first, count)) in enumerate(post_msgs.items()):
            layer = {a: (7 if d[a] == 1 else 0) for a in (1, 2)}
            if d in face_pops:
                listed = face_pops[d]
            else:
                listed = [lattice.index(d)]
            if d[0] != 0 and d[1] == 0 and d[2] == 0:
                acc = jnp.zeros((8, 128), f32)
                from_lane = 127 if d[0] == 1 else 0
                for k, i in enumerate(listed):
                    for z in range(8):
                        spot = k * 8 + z
                        turned = pltpu.roll(posts[i, tile_rows(z), :], (spot - from_lane) % 128, 1)
                        acc = jnp.where(lane == spot, turned, acc)
                psend[r, tile_rows(first), :] = acc
            elif d[2] != 0:
                for k, i in enumerate(listed):
                    psend[r, tile_rows(first + k), :] = posts[i, tile_rows(layer[2]), :]
            else:
                for k, i in enumerate(listed):
                    psend[r, tile_rows(first + k), :] = posts[i, pl.ds(layer[1], 8, stride=8), :]
            part = pl.ds(first * 8, count * 8)
            copies[d] = copy(r * N_POST + number, psend.at[r, part], precv.at[r, part], d)
        return copies

    def pull(r, i):
        cx, cy, cz = lattice[i]
        far = 127 if cx == 1 else 0

        def halo(d):
            first, count = post_msgs[d]
            k = face_pops[d].index(i) if d in face_pops and d[0] == 0 else 0
            return first + k

        def x_shift(value, beyond):
            return pltpu.roll(jnp.where(lane == far, beyond, value), cx % 128, 1)

        def y_shift(value, row):
            edge = 0 if cy == 1 else 7
            return jnp.where(sub == edge, row, pltpu.roll(value, cy % 8, 0))

        wanted = [z - cz for z in range(8)]
        planes = {z: posts[i, tile_rows(z), :] for z in range(8) if z in wanted}
        outer = None
        if cz != 0:
            outer = precv[r, tile_rows(halo((0, 0, cz))), :]
        if cx != 0:
            packed = precv[r, tile_rows(post_msgs[(cx, 0, 0)][0]), :]
            k = face_pops[(cx, 0, 0)].index(i)
            for z in planes:
                planes[z] = x_shift(planes[z], pltpu.roll(packed, (far - (k * 8 + z)) % 128, 1))
            if cz != 0:
                outer = x_shift(outer, precv[r, tile_rows(halo((cx, 0, cz))), :])
        if cy != 0:
            place = halo((0, cy, 0))
            if cx != 0:
                side = x_shift(precv[r, tile_rows(place), :], precv[r, tile_rows(halo((cx, cy, 0))), :])
                for z in planes:
                    planes[z] = y_shift(planes[z], side[z : z + 1, :])
            else:
                for z in planes:
                    planes[z] = y_shift(planes[z], precv[r, pl.ds(place * 8 + z, 1), :])
            if cz != 0:
                row = halo((0, cy, cz)) * 8 + (7 if cy == 1 else 0)
                outer = y_shift(outer, precv[r, pl.ds(row, 1), :])
        out = [planes[z] if z in planes else outer for z in wanted]
        if cz == 1:
            out[0] = jnp.where(at_bottom, posts[opposite[i], tile_rows(0), :], out[0])
        if cz == -1:
            out[7] = jnp.where(at_top, posts[opposite[i], tile_rows(7), :], out[7])
        return out

    def stream(r, copies):
        for made in copies.values():
            made.wait_recv()
        for i in range(19):
            out = pull(r, i)
            for z in range(8):
                state[r, i, tile_rows(z), :] = out[z]

    def prepare():
        for axis in range(3):
            angle = drop_frac[axis] * (0.5 * math.pi)
            sine = jnp.sin(angle)
            cosine = jnp.cos(angle)
            taps[axis * 4 + 0] = 0.25 - 0.25 * sine
            taps[axis * 4 + 1] = 0.25 + 0.25 * cosine
            taps[axis * 4 + 2] = 0.25 + 0.25 * sine
            taps[axis * 4 + 3] = 0.25 - 0.25 * cosine
        cells = home[...]
        homes[0] = (cells & 127) - 1
        homes[1] = ((cells >> 7) & 7) - 1
        homes[2] = (cells >> 10) - 1

    def picked(offset, weight):
        zero = jnp.zeros(offset.shape, f32)
        return jnp.where(
            offset == 0,
            weight[0],
            jnp.where(offset == 1, weight[1], jnp.where(offset == 2, weight[2], jnp.where(offset == 3, weight[3], zero))),
        )

    def build_weights(low, high):
        rows16 = lax.broadcasted_iota(jnp.int32, (16, 128), 0)

        @pl.loop(low, high)
        def _(p):
            for j in range(2):
                block = pl.ds(2 * p + j, 1)
                lanes = pl.ds(j * 128, 128)
                first = homes[0, block, :]
                weight = [taps[k, block, :] for k in range(4)]
                for t in range(9):
                    if t < 8:
                        cell = rows16 + t * 16
                    else:
                        cell = jnp.where(rows16 < 2, rows16 + 128, jnp.where(rows16 == 2, -1, -1000))
                    value = picked(cell - first, weight)
                    high_part = value.astype(bf16)
                    whi[p, pl.ds(t * 16, 16), lanes] = high_part
                    wlo[p, pl.ds(t * 16, 16), lanes] = (value - high_part.astype(f32)).astype(bf16)
            whi[p, pl.ds(144, 112), :] = jnp.zeros((112, 256), bf16)
            wlo[p, pl.ds(144, 112), :] = jnp.zeros((112, 256), bf16)

    collide(pops)
    pl.semaphore_wait(barrier, len(all_dirs))
    first_copies = send_posts(0)
    prepare()
    build_weights(0, PAIRS // 2)
    stream(0, first_copies)
    collide(state.at[0])
    second_copies = send_posts(1)
    build_weights(PAIRS // 2, PAIRS)
    stream(1, second_copies)
    state_copy = pltpu.make_async_copy(state.at[1], state_hbm, out_sem)
    state_copy.start()

    for z in range(8):
        values = [state[1, i, tile_rows(z), :] for i in range(19)]
        flow = macroscopic(values)[1]
        for c in range(3):
            vmain[tile_rows(c * 8 + z), :] = flow[c]

    def sent_tile(region, k):
        dy, dz = region
        if region == (0, 0):
            return vmain[tile_rows(k), :]
        if dz == 0:
            start = (k // 2) * 64 + k % 2 if dy == -1 else k * 64 + 7
            return vmain[pl.ds(start, 8, stride=8), :]
        if dy == 0:
            tile = (k // 2) * 8 + k % 2 if dz == -1 else k * 8 + 7
            return vmain[tile_rows(tile), :]
        acc = jnp.zeros((8, 128), f32)
        for r, (c, y, z) in enumerate(corner_rows(region)[k * 8 : k * 8 + 8]):
            acc = jnp.where(sub == r, vmain[pl.ds(c * 64 + z * 8 + y, 1), :], acc)
        return acc

    v_copies = []
    number = 2 * N_POST
    for n, region in enumerate(region_list):
        first, count = region_span = regions[region]
        ahead = jnp.zeros((8, 128), f32)
        behind = jnp.zeros((8, 128), f32)
        for k in range(count):
            value = sent_tile(region, k)
            if region != (0, 0):
                vsend[tile_rows(first - 24 + k), :] = value
            behind = jnp.where((lane >> 1) == k, pltpu.roll(value, (2 * k) % 128, 1), behind)
            ahead = jnp.where(lane == k, pltpu.roll(value, (k - 127) % 128, 1), ahead)
        pksend[0, tile_rows(n), :] = behind
        pksend[1, tile_rows(n), :] = ahead
        if region != (0, 0):
            part = pl.ds((first - 24) * 8, count * 8)
            v_copies.append(
                copy(number, vsend.at[part], vmain.at[pl.ds(first * 8, count * 8)], (0,) + region)
            )
            number += 1
        for side, dx in ((0, -1), (1, 1)):
            part = pl.ds(n * 8, 8)
            v_copies.append(copy(number, pksend.at[side, part], pkrecv.at[side, part], (dx,) + region))
            number += 1

    facc[...] = jnp.zeros((ROWS, 256), f32)
    vmain[tile_rows(47), :] = jnp.zeros((8, 128), f32)
    vhalo[tile_rows(47), :] = jnp.zeros((8, 128), f32)
    for made in v_copies:
        made.wait_recv()
    for n, region in enumerate(region_list):
        first, count = regions[region]
        behind = pkrecv[0, tile_rows(n), :]
        ahead = pkrecv[1, tile_rows(n), :]
        for k in range(count):
            value = jnp.where(lane < 2, pltpu.roll(behind, (-2 * k) % 128, 1), 0.0)
            value = jnp.where(lane == 2, pltpu.roll(ahead, (2 - k) % 128, 1), value)
            vhalo[tile_rows(first + k), :] = value
    for t in range(ROWS // 16):
        rows = pl.ds(t * 16, 16)
        for source, lanes in ((vmain, pl.ds(0, 128)), (vhalo, pl.ds(128, 128))):
            value = source[rows, :]
            high_part = value.astype(bf16)
            vhi[rows, lanes] = high_part
            vlo[rows, lanes] = (value - high_part.astype(f32)).astype(bf16)

    @pl.loop(0, PAIRS)
    def _(p):
        w_high = whi[p]
        w_low = wlo[p]
        v_high = vhi[...]
        sampled_all = (
            jnp.dot(v_high, w_high, preferred_element_type=f32)
            + jnp.dot(v_high, w_low, preferred_element_type=f32)
            + jnp.dot(vlo[...], w_high, preferred_element_type=f32)
        )
        for j in range(2):
            lanes = pl.ds(j * 128, 128)
            b = 2 * p + j
            block = pl.ds(b, 1)
            t1 = sampled_all[:, j * 128 : (j + 1) * 128]

            def tile(t):
                return t1[t * 8 : t * 8 + 8, :]

            hy = homes[1, block, :]
            hz = homes[2, block, :]
            wy = [taps[4 + k, block, :] for k in range(4)]
            wz = [taps[8 + k, block, :] for k in range(4)]
            y_main = picked(sub - hy, wy)
            z_main = picked(sub - hz, wz)
            y_out = [picked(y - hy, wy) for y in (8, 9, -1)]
            z_out = [picked(z - hz, wz) for z in (8, 9, -1)]
            z_out = [jnp.where(at_top, 0.0, z_out[0]), jnp.where(at_top, 0.0, z_out[1]), jnp.where(at_bottom, 0.0, z_out[2])]
            even = (sub & 1) == 0
            y_pair = jnp.where(even, y_out[0], y_out[1])
            u_main = [y_main * z_main[z : z + 1, :] for z in range(8)]
            u_y = [z_main * y_out[k] for k in range(3)]
            u_z = [y_main * z_out[k] for k in range(3)]
            both = y_pair * jnp.where((sub & 2) == 0, z_out[0], z_out[1])
            u42 = both
            u43 = jnp.where(sub < 4, both, 0.0)
            u44 = jnp.where(sub < 6, y_out[2] * jnp.where(even, z_out[0], z_out[1]), 0.0)
            u45 = jnp.where(sub < 6, y_pair * z_out[2], 0.0)
            u46 = jnp.where(sub < 3, y_out[2] * z_out[2] + jnp.zeros((8, 128), f32), 0.0)
            p42 = tile(42) * u42
            p43 = tile(43) * u43
            p445 = tile(44) * u44 + tile(45) * u45
            p46 = tile(46) * u46
            alive = lax.broadcasted_iota(jnp.int32, (1, 128), 1) < counts[b]
            pushes = []
            rows = []
            for c in range(3):
                acc = jnp.where((sub >> 1) == c, p445, 0.0) + jnp.where(sub == c, p46, 0.0)
                if c < 2:
                    acc = acc + jnp.where((sub >> 2) == c, p42, 0.0)
                else:
                    acc = acc + p43
                for z in range(8):
                    acc = acc + tile(c * 8 + z) * u_main[z]
                acc = acc + tile(24 + c * 2) * u_y[0] + tile(25 + c * 2) * u_y[1] + tile(30 + c) * u_y[2]
                acc = acc + tile(33 + c * 2) * u_z[0] + tile(34 + c * 2) * u_z[1] + tile(39 + c) * u_z[2]
                sampled = jnp.sum(acc, axis=0, keepdims=True)
                speed = drop_vel[c, block, :]
                moved = speed + relax * (sampled - speed)
                pushes.append(jnp.where(alive, couple * (moved - sampled), 0.0))
                rows.append(jnp.where(alive, moved, 0.0))
            for c in range(3):
                rows.append(jnp.where(alive, drop_frac[c, block, :], 0.0) + rows[c])
            block_state = jnp.zeros((8, 128), f32)
            for c in range(6):
                block_state = jnp.where(sub == c, rows[c], block_state)
            states[pl.ds(pl.multiple_of(b * 8, 8), 8), :] = block_state

            by_half = jnp.where((sub >> 1) == 0, pushes[0], jnp.where((sub >> 1) == 1, pushes[1], pushes[2]))
            sources = [pushes[c] * u_main[z] for c in range(3) for z in range(8)]
            sources += [pushes[c] * u_y[k] for c in range(3) for k in range(2)]
            sources += [pushes[c] * u_y[2] for c in range(3)]
            sources += [pushes[c] * u_z[k] for c in range(3) for k in range(2)]
            sources += [pushes[c] * u_z[2] for c in range(3)]
            sources.append(jnp.where(sub < 4, pushes[0], pushes[1]) * u42)
            sources.append(pushes[2] * u43)
            sources.append(by_half * u44)
            sources.append(by_half * u45)
            sources.append(jnp.where(sub == 0, pushes[0], jnp.where(sub == 1, pushes[1], pushes[2])) * u46)
            sources.append(jnp.zeros((8, 128), f32))
            for t in range(ROWS // 16):
                value = jnp.concatenate([sources[2 * t], sources[2 * t + 1]], axis=0)
                high_part = value.astype(bf16)
                shi[pl.ds(t * 16, 16), lanes] = high_part
                slo[pl.ds(t * 16, 16), lanes] = (value - high_part.astype(f32)).astype(bf16)

        def over_droplets(source, weight):
            return lax.dot_general(source, weight, (((1,), (1,)), ((), ())), preferred_element_type=f32)

        s_high = shi[...]
        facc[...] += over_droplets(s_high, w_high) + over_droplets(s_high, w_low) + over_droplets(slo[...], w_high)

    codes = [dest[b] for b in range(BLOCKS)]
    wide = lax.broadcasted_iota(jnp.int32, (8, 128), 1)
    owner = wide >> 3
    code = jnp.zeros((8, 128), jnp.int32)
    for b in range(BLOCKS):
        code = jnp.where(owner == b, codes[b], code)
    rank = jnp.zeros((8, 128), jnp.int32)
    for b in range(BLOCKS):
        rank = rank + jnp.where((code == codes[b]) & (owner > b), 1, 0)
    lanes_of = jnp.where(code < 13, code, code - 1) * 2 + rank
    key = jnp.where(code == 13, -1, lanes_of * 8 + (wide & 7))[0:1, :]
    value = states[...]
    part_0 = value.astype(bf16)
    value = value - part_0.astype(f32)
    part_1 = value.astype(bf16)
    part_2 = (value - part_1.astype(f32)).astype(bf16)
    chosen = jnp.where(lax.broadcasted_iota(jnp.int32, (416, 128), 0) == key, 1.0, 0.0).astype(bf16)
    outbox[...] = (
        jnp.dot(chosen, part_0, preferred_element_type=f32)
        + jnp.dot(chosen, part_1, preferred_element_type=f32)
        + jnp.dot(chosen, part_2, preferred_element_type=f32)
    )
    h_copies = []
    for n, d in enumerate(all_dirs):
        part = pl.ds(n * 16, 16)
        h_copies.append(copy(number, outbox.at[part], inbox.at[part], d))
        number += 1

    f_copies = []
    for n, region in enumerate(region_list):
        first, count = regions[region]
        behind = jnp.zeros((8, 128), f32)
        ahead = jnp.zeros((8, 128), f32)
        for k in range(count):
            rows = tile_rows(first + k)
            if region != (0, 0):
                fsend[tile_rows(first - 24 + k), :] = facc[rows, 0:128]
            beyond = facc[rows, 128:256]
            behind = jnp.where((lane >> 1) == k, pltpu.roll(beyond, (2 * k) % 128, 1), behind)
            ahead = jnp.where(lane == k, pltpu.roll(beyond, (k - 2) % 128, 1), ahead)
        fpsend[0, tile_rows(n), :] = behind
        fpsend[1, tile_rows(n), :] = ahead
        back = (-region[0], -region[1])
        if region != (0, 0):
            part = pl.ds((first - 24) * 8, count * 8)
            f_copies.append(copy(number, fsend.at[part], frecv.at[part], (0,) + back))
            number += 1
        for side, dx in ((0, -1), (1, 1)):
            part = pl.ds(n * 8, 8)
            f_copies.append(copy(number, fpsend.at[side, part], fprecv.at[side, part], (-dx,) + back))
            number += 1

    stay_rows = lax.broadcasted_iota(jnp.int32, (16, 128), 0)
    stays = jnp.zeros((16, 128), jnp.int32)
    for b in range(BLOCKS):
        stays = jnp.where(stay_rows == b, codes[b], stays)
    for c in range(6):
        arrived[c, pl.ds(0, 16), :] = jnp.where(stays == 13, states[pl.ds(c, 16, stride=8), :], 0.0)

    for made in f_copies:
        made.wait_recv()
    for n, region in enumerate(region_list):
        first, count = regions[region]
        behind = fprecv[0, tile_rows(n), :]
        ahead = fprecv[1, tile_rows(n), :]
        for k in range(count):
            value = jnp.where(lane < 2, pltpu.roll(behind, (-2 * k) % 128, 1), 0.0)
            value = jnp.where(lane == 127, pltpu.roll(ahead, (127 - k) % 128, 1), value)
            rows = tile_rows(first + k)
            if region == (0, 0):
                facc[rows, 0:128] += value
            else:
                vhalo[rows, :] = frecv[tile_rows(first - 24 + k), :] + value

    def row_of(t, r):
        return vhalo[pl.ds(t * 8 + r, 1), :]

    def corner_row(region, c, y, z):
        return row_of(regions[region][0], corner_rows(region).index((c, y, z)))

    for c in range(3):
        for z in range(8):
            total = facc[tile_rows(c * 8 + z), 0:128]
            lines = [row_of(24 + c * 2, z), row_of(25 + c * 2, z), row_of(30 + c, z)]
            if z < 2 or z == 7:
                if z < 2:
                    total = total + vhalo[tile_rows(33 + c * 2 + z), :]
                    low, high = (-1, -1), (1, -1)
                else:
                    total = total + vhalo[tile_rows(39 + c), :]
                    low, high = (-1, 1), (1, 1)
                lines[0] = lines[0] + corner_row(low, c, 0, z)
                lines[1] = lines[1] + corner_row(low, c, 1, z)
                lines[2] = lines[2] + corner_row(high, c, 7, z)
            beside = jnp.where(sub == 0, lines[0], jnp.where(sub == 1, lines[1], jnp.where(sub == 7, lines[2], 0.0)))
            force[c, tile_rows(z), :] = total + beside

    for made in h_copies:
        made.wait_recv()
    for c in range(6):
        arrived[c, pl.ds(16, 52), :] = inbox[pl.ds(c, 52, stride=8), :]
    state_copy.wait()
    for made in started:
        made.wait_send()


def solution(mesh):
    sizes = tuple(mesh.shape[a] for a in ("gx", "gy", "gz"))

    def body(*refs):
        kernel(sizes, *refs)

    def local(pops, coarse_pops, interface, drop_vel, drop_frac, home, counts, dest):
        vmem = pl.BlockSpec(memory_space=pltpu.VMEM)
        smem = pl.BlockSpec(memory_space=pltpu.SMEM)
        state, force, arrived = pl.pallas_call(
            body,
            out_shape=(
                jax.ShapeDtypeStruct((19, 64, 128), f32),
                jax.ShapeDtypeStruct((3, 64, 128), f32),
                jax.ShapeDtypeStruct((6, 68, 128), f32),
            ),
            in_specs=[vmem] * 6 + [smem] * 2,
            out_specs=(pl.BlockSpec(memory_space=pl.ANY), vmem, vmem),
            scratch_shapes=[
                pltpu.VMEM((19, 64, 128), f32),
                pltpu.VMEM((2, 19, 64, 128), f32),
                pltpu.VMEM((2, POST_TILES * 8, 128), f32),
                pltpu.VMEM((2, POST_TILES * 8, 128), f32),
                pltpu.VMEM((ROWS, 128), f32),
                pltpu.VMEM((ROWS, 128), f32),
                pltpu.VMEM((24 * 8, 128), f32),
                pltpu.VMEM((2, 72, 128), f32),
                pltpu.VMEM((2, 72, 128), f32),
                pltpu.VMEM((ROWS, 256), bf16),
                pltpu.VMEM((ROWS, 256), bf16),
                pltpu.VMEM((PAIRS, 256, 256), bf16),
                pltpu.VMEM((PAIRS, 256, 256), bf16),
                pltpu.VMEM((12, 16, 128), f32),
                pltpu.VMEM((3, 16, 128), jnp.int32),
                pltpu.VMEM((ROWS, 256), bf16),
                pltpu.VMEM((ROWS, 256), bf16),
                pltpu.VMEM((ROWS, 256), f32),
                pltpu.VMEM((24 * 8, 128), f32),
                pltpu.VMEM((24 * 8, 128), f32),
                pltpu.VMEM((2, 72, 128), f32),
                pltpu.VMEM((2, 72, 128), f32),
                pltpu.VMEM((BLOCKS * 8, 128), f32),
                pltpu.VMEM((416, 128), f32),
                pltpu.VMEM((416, 128), f32),
                pltpu.SemaphoreType.DMA((N_MSG,)),
                pltpu.SemaphoreType.DMA((N_MSG,)),
                pltpu.SemaphoreType.DMA,
            ],
            compiler_params=pltpu.CompilerParams(collective_id=0, has_side_effects=True),
            name="channel",
        )(
            pops.reshape(19, 64, 128),
            coarse_pops,
            interface,
            drop_vel,
            drop_frac,
            home,
            counts,
            dest,
        )
        return state.reshape(19, 8, 8, 128), force.reshape(3, 8, 8, 128), arrived

    return jax.shard_map(
        local,
        mesh=mesh,
        in_specs=(
            P(None, "gz", "gy", "gx"),
            P(None, "gz", "gy", "gx"),
            P("gz", "gy", "gx"),
            P(None, ("gx", "gy", "gz"), None),
            P(None, ("gx", "gy", "gz"), None),
            P(("gx", "gy", "gz"), None),
            P(("gx", "gy", "gz")),
            P(("gx", "gy", "gz")),
        ),
        out_specs=(
            P(None, "gz", "gy", "gx"),
            P(None, "gz", "gy", "gx"),
            P(None, ("gx", "gy", "gz"), None),
        ),
        check_vma=False,
    )
```

```python
import math

import jax
import jax.numpy as jnp
import numpy as np
from jax import lax
from jax.experimental import pallas as pl
from jax.experimental.pallas import tpu as pltpu
from jax.sharding import PartitionSpec as P

lattice = [
    (0, 0, 0), (1, 0, 0), (-1, 0, 0), (0, 1, 0), (0, -1, 0), (0, 0, 1), (0, 0, -1),
    (1, 1, 0), (-1, -1, 0), (1, -1, 0), (-1, 1, 0), (1, 0, 1), (-1, 0, -1), (1, 0, -1),
    (-1, 0, 1), (0, 1, 1), (0, -1, -1), (0, 1, -1), (0, -1, 1),
]
weights_table = [1.0 / 3.0] + [1.0 / 18.0] * 6 + [1.0 / 36.0] * 12
opposite = [0, 2, 1, 4, 3, 6, 5, 8, 7, 10, 9, 12, 11, 14, 13, 16, 15, 18, 17]
inverse_tau = 0.8
relax = 0.5
couple = 8.0
f32 = jnp.float32
bf16 = jnp.bfloat16

face_pops = {}
for axis in range(3):
    for sign in (1, -1):
        d = [0, 0, 0]
        d[axis] = sign
        face_pops[tuple(d)] = [i for i in range(19) if lattice[i][axis] == sign]
post_msgs = {}
tiles = 0
for i in list(range(7, 19)) + [3, 4, 5, 6, 1, 2]:
    c = lattice[i]
    count = 1 if (abs(c[0]) + abs(c[1]) + abs(c[2]) > 1 or c[0] != 0) else 5
    post_msgs[c] = (tiles, count)
    tiles += count
POST_TILES = tiles

regions = {
    (0, 0): (0, 24),
    (-1, 0): (24, 6),
    (1, 0): (30, 3),
    (0, -1): (33, 6),
    (0, 1): (39, 3),
    (-1, -1): (42, 2),
    (1, -1): (44, 1),
    (-1, 1): (45, 1),
    (1, 1): (46, 1),
}
region_list = list(regions)[::-1]
ROWS = 48 * 8
all_dirs = [(x, y, z) for z in (-1, 0, 1) for y in (-1, 0, 1) for x in (-1, 0, 1) if (x, y, z) != (0, 0, 0)]
far_first = sorted(all_dirs, key=lambda d: -abs(d[0]) - abs(d[1]) - abs(d[2]))
U_TILES = 19
WIDE = 2048
N_POST = 18
N_MSG = 2 * N_POST + 3 * 26
PAIRS = 8
BLOCKS = 16
UNROLL = 4
GROUP = 12


def corner_rows(region):
    dy, dz = region
    ys = [7] if dy == 1 else [0, 1]
    zs = [7] if dz == 1 else [0, 1]
    return [(c, y, z) for c in range(3) for z in zs for y in ys]


def tile_rows(t):
    return pl.ds(t * 8, 8)


def kernel(
    sizes,
    pops_hbm, coarse_hbm, interface_hbm, drop_vel_hbm, drop_frac_hbm, home_hbm, counts_hbm, dest_hbm,
    state_out, force, arrived,
    pops, coarse, interface, drop_vel, drop_frac, home, counts, dest,
    posts, state_mid, psend, precv, vmain, vsend, pksend, pkrecv, va, vb, weights,
    taps, homes, spread_weights, tmain, shi, slo, f_main, f_beyond, fsend, frecv, fpsend, fprecv, states, outbox, inbox,
    send_sem, recv_sem, in_sem,
):
    n_x, n_y, n_z = sizes
    me = (lax.axis_index("gx"), lax.axis_index("gy"), lax.axis_index("gz"))
    level = me[2]
    at_bottom = level == 0
    at_top = level == n_z - 1

    def moved_by(axis, step, size):
        if step == 0:
            return me[axis]
        return lax.rem(me[axis] + (step + size), size)

    coords = {
        (axis, step): moved_by(axis, step, size)
        for axis, size in enumerate(sizes)
        for step in (-1, 0, 1)
    }

    def device(d):
        return {"gx": coords[0, d[0]], "gy": coords[1, d[1]], "gz": coords[2, d[2]]}

    lane = lax.broadcasted_iota(jnp.int32, (8, 128), 1)
    sub = lax.broadcasted_iota(jnp.int32, (8, 128), 0)

    third = (lane * 171) >> 9
    outer_low = lane - third * 3 == 0
    started = []

    def copy(index, src, dst, d):
        made = pltpu.make_async_remote_copy(
            src_ref=src,
            dst_ref=dst,
            send_sem=send_sem.at[index],
            recv_sem=recv_sem.at[index],
            device_id=device(d),
            device_id_type=pl.DeviceIdType.MESH,
        )
        made.start()
        started.append(made)
        return made

    loads = []
    for n, (src, dst) in enumerate(
        (
            (pops_hbm, pops),
            (coarse_hbm, coarse),
            (interface_hbm, interface),
            (drop_vel_hbm, drop_vel),
            (drop_frac_hbm, drop_frac),
            (home_hbm, home),
            (counts_hbm, counts),
            (dest_hbm, dest),
        )
    ):
        loads.append(pltpu.make_async_copy(src, dst, in_sem.at[n]))
        loads[-1].start()
    barrier = pltpu.get_barrier_semaphore()
    for d in far_first:
        pl.semaphore_signal(barrier, inc=1, device_id=device(d), device_id_type=pl.DeviceIdType.MESH)

    def macroscopic(values):
        plus = {i: values[i] + values[i + 1] for i in range(1, 19, 2)}
        minus = {i: values[i] - values[i + 1] for i in range(1, 19, 2)}
        axes = plus[1] + plus[3] + plus[5]
        edges = (plus[7] + plus[9]) + (plus[11] + plus[13]) + (plus[15] + plus[17])
        density = values[0] * weights_table[0] + axes * weights_table[1] + edges * weights_table[7]
        inverse = 1.0 / density
        near, far = weights_table[1] * inverse, weights_table[7] * inverse
        flow = [
            minus[1] * near + ((minus[7] + minus[9]) + (minus[11] + minus[13])) * far,
            minus[3] * near + ((minus[7] - minus[9]) + (minus[15] + minus[17])) * far,
            minus[5] * near + ((minus[11] - minus[13]) + (minus[15] - minus[17])) * far,
        ]
        return density, flow

    def collide(source):
        @pl.loop(0, 8)
        def _(z):
            rows = pl.ds(pl.multiple_of(z * 8, 8), 8)
            values = [source[i, rows, :] for i in range(19)]
            density, flow = macroscopic(values)
            square = flow[0] * flow[0] + flow[1] * flow[1] + flow[2] * flow[2]
            inside = interface[z] == 1
            scaled = density * inverse_tau
            base = scaled - square * (1.5 * scaled)
            first, second = scaled * 3.0, scaled * 4.5

            def put(i, balance):
                relaxed = values[i] * (1.0 - inverse_tau) + balance
                posts[i, rows, :] = jnp.where(inside, coarse[i, z].astype(f32), relaxed)

            put(0, base)
            for i in range(1, 19, 2):
                along = None
                for axis in range(3):
                    sign = lattice[i][axis]
                    if sign == 1:
                        along = flow[axis] if along is None else along + flow[axis]
                    if sign == -1:
                        along = along - flow[axis]
                even = base + along * along * second
                odd = along * first
                put(i, even + odd)
                put(i + 1, even - odd)

    def send_posts(r):
        copies = {}
        for number, (d, (first, count)) in enumerate(post_msgs.items()):
            layer = {a: (7 if d[a] == 1 else 0) for a in (1, 2)}
            if d in face_pops:
                listed = face_pops[d]
            else:
                listed = [lattice.index(d)]
            if d[0] != 0 and d[1] == 0 and d[2] == 0:
                acc = jnp.zeros((8, 128), f32)
                from_lane = 127 if d[0] == 1 else 0
                for k, i in enumerate(listed):
                    for z in range(8):
                        spot = k * 8 + z
                        turned = pltpu.roll(posts[i, tile_rows(z), :], (spot - from_lane) % 128, 1)
                        acc = jnp.where(lane == spot, turned, acc)
                psend[r, tile_rows(first), :] = acc
            elif d[2] != 0:
                for k, i in enumerate(listed):
                    psend[r, tile_rows(first + k), :] = posts[i, tile_rows(layer[2]), :]
            else:
                for k, i in enumerate(listed):
                    psend[r, tile_rows(first + k), :] = posts[i, pl.ds(layer[1], 8, stride=8), :]
            part = pl.ds(first * 8, count * 8)
            copies[d] = copy(r * N_POST + number, psend.at[r, part], precv.at[r, part], d)
        return copies

    def pull(r, i):
        cx, cy, cz = lattice[i]
        far = 127 if cx == 1 else 0

        def halo(d):
            first, count = post_msgs[d]
            k = face_pops[d].index(i) if d in face_pops and d[0] == 0 else 0
            return first + k

        def x_shift(value, beyond):
            return pltpu.roll(jnp.where(lane == far, beyond, value), cx % 128, 1)

        def y_shift(value, row):
            edge = 0 if cy == 1 else 7
            return jnp.where(sub == edge, row, pltpu.roll(value, cy % 8, 0))

        wanted = [z - cz for z in range(8)]
        planes = {z: posts[i, tile_rows(z), :] for z in range(8) if z in wanted}
        outer = None
        if cz != 0:
            outer = precv[r, tile_rows(halo((0, 0, cz))), :]
        if cx != 0:
            packed = precv[r, tile_rows(post_msgs[(cx, 0, 0)][0]), :]
            k = face_pops[(cx, 0, 0)].index(i)
            for z in planes:
                planes[z] = x_shift(planes[z], pltpu.roll(packed, (far - (k * 8 + z)) % 128, 1))
            if cz != 0:
                outer = x_shift(outer, precv[r, tile_rows(halo((cx, 0, cz))), :])
        if cy != 0:
            place = halo((0, cy, 0))
            if cx != 0:
                side = x_shift(precv[r, tile_rows(place), :], precv[r, tile_rows(halo((cx, cy, 0))), :])
                for z in planes:
                    planes[z] = y_shift(planes[z], side[z : z + 1, :])
            else:
                for z in planes:
                    planes[z] = y_shift(planes[z], precv[r, pl.ds(place * 8 + z, 1), :])
            if cz != 0:
                row = halo((0, cy, cz)) * 8 + (7 if cy == 1 else 0)
                outer = y_shift(outer, precv[r, pl.ds(row, 1), :])
        out = [planes[z] if z in planes else outer for z in wanted]
        if cz == 1:
            out[0] = jnp.where(at_bottom, posts[opposite[i], tile_rows(0), :], out[0])
        if cz == -1:
            out[7] = jnp.where(at_top, posts[opposite[i], tile_rows(7), :], out[7])
        return out

    def stream(r, copies, into):
        for made in copies.values():
            made.wait_recv()
        for i in range(19):
            out = pull(r, i)
            for z in range(8):
                into[i, tile_rows(z), :] = out[z]

    def prepare():
        for axis in range(3):
            angle = drop_frac[axis] * (0.5 * math.pi)
            sine = jnp.sin(angle)
            cosine = jnp.cos(angle)
            taps[axis * 4 + 0] = 0.25 - 0.25 * sine
            taps[axis * 4 + 1] = 0.25 + 0.25 * cosine
            taps[axis * 4 + 2] = 0.25 + 0.25 * sine
            taps[axis * 4 + 3] = 0.25 - 0.25 * cosine
        cells = home[...]
        homes[0] = (cells & 127) - 1
        homes[1] = ((cells >> 7) & 7) - 1
        homes[2] = (cells >> 10) - 1

    def picked(offset, weight):
        zero = jnp.zeros(offset.shape, f32)
        return jnp.where(
            offset == 0,
            weight[0],
            jnp.where(offset == 1, weight[1], jnp.where(offset == 2, weight[2], jnp.where(offset == 3, weight[3], zero))),
        )

    rows16 = lax.broadcasted_iota(jnp.int32, (16, 128), 0)

    def build_x_weights():
        @pl.loop(0, BLOCKS)
        def _(b):
            block = pl.ds(b, 1)
            lanes = pl.ds(pl.multiple_of(b * 128, 128), 128)
            first = homes[0, block, :]
            weight = [taps[k, block, :] for k in range(4)]
            for t in range(8):
                value = picked(rows16 + t * 16 - first, weight)
                high_part = value.astype(bf16)
                weights[pl.ds(t * 16, 16), lanes] = high_part
                weights[pl.ds(128 + t * 16, 16), lanes] = (value - high_part.astype(f32)).astype(bf16)
            def outside(at):
                row = rows16 - at
                cell = jnp.where(row == 0, -1, jnp.where(row == 1, 128, jnp.where(row == 2, 129, -1000)))
                return picked(cell - first, weight)

            value = outside(0)
            high_part = value.astype(bf16)
            weights[pl.ds(256, 16), lanes] = high_part
            weights[pl.ds(272, 16), lanes] = jnp.zeros((16, 128), bf16)
            weights[pl.ds(288, 16), lanes] = outside(8).astype(bf16)
            weights[pl.ds(304, 32), lanes] = jnp.zeros((32, 128), bf16)
            weights[pl.ds(336, 16), lanes] = (value - high_part.astype(f32)).astype(bf16)
            weights[pl.ds(352, 32), lanes] = jnp.zeros((32, 128), bf16)

    def build_yz_weights():
        @pl.loop(0, BLOCKS)
        def _(b):
            block = pl.ds(b, 1)
            hy = homes[1, block, :]
            hz = homes[2, block, :]
            wy = [taps[4 + k, block, :] for k in range(4)]
            wz = [taps[8 + k, block, :] for k in range(4)]
            y_main = picked(sub - hy, wy)
            z_main = picked(sub - hz, wz)
            y_out = [picked(y - hy, wy) for y in (8, 9, -1)]
            z_out = [picked(z - hz, wz) for z in (8, 9, -1)]
            z_out = [jnp.where(at_top, 0.0, z_out[0]), jnp.where(at_top, 0.0, z_out[1]), jnp.where(at_bottom, 0.0, z_out[2])]
            even = (sub & 1) == 0
            y_pair = jnp.where(even, y_out[0], y_out[1])
            z_pair = jnp.where(even, z_out[0], z_out[1])
            both = y_pair * jnp.where((sub & 2) == 0, z_out[0], z_out[1])
            made = [y_main * z_main[z : z + 1, :] for z in range(8)]
            made += [z_main * y_out[k] for k in range(3)]
            made += [y_main * z_out[k] for k in range(3)]
            made.append(both)
            made.append(jnp.where(sub < 4, both, 0.0))
            made.append(jnp.where(sub < 6, y_out[2] * z_pair, 0.0))
            made.append(jnp.where(sub < 6, y_pair * z_out[2], 0.0))
            made.append(jnp.where(sub < 3, y_out[2] * z_out[2], 0.0))
            for t in range(U_TILES):
                spread_weights[b, tile_rows(t), :] = made[t]

    for made in loads[:3]:
        made.wait()
    collide(pops)
    pl.semaphore_wait(barrier, len(all_dirs))
    first_copies = send_posts(0)
    stream(0, first_copies, state_mid)
    collide(state_mid)
    second_copies = send_posts(1)
    for made in loads[3:]:
        made.wait()
    prepare()
    build_x_weights()
    build_yz_weights()
    stream(1, second_copies, state_out)

    for z in range(8):
        values = [state_out[i, tile_rows(z), :] for i in range(19)]
        flow = macroscopic(values)[1]
        for c in range(3):
            vmain[tile_rows(c * 8 + z), :] = flow[c]

    def sent_tile(region, k):
        dy, dz = region
        if region == (0, 0):
            return vmain[tile_rows(k), :]
        if dz == 0:
            start = (k // 2) * 64 + k % 2 if dy == -1 else k * 64 + 7
            return vmain[pl.ds(start, 8, stride=8), :]
        if dy == 0:
            tile = (k // 2) * 8 + k % 2 if dz == -1 else k * 8 + 7
            return vmain[tile_rows(tile), :]
        acc = jnp.zeros((8, 128), f32)
        for r, (c, y, z) in enumerate(corner_rows(region)[k * 8 : k * 8 + 8]):
            acc = jnp.where(sub == r, vmain[pl.ds(c * 64 + z * 8 + y, 1), :], acc)
        return acc

    v_copies = []
    number = 2 * N_POST
    for n, region in enumerate(region_list):
        first, count = regions[region]
        packed = jnp.zeros((8, 128), f32)
        for k in range(count):
            value = sent_tile(region, k)
            if region != (0, 0):
                vsend[tile_rows(first - 24 + k), :] = value
            packed = jnp.where(third == k, pltpu.roll(value, 3 * k + 1, 1), packed)
        pksend[tile_rows(n), :] = packed
        for side, dx in ((0, -1), (1, 1)):
            part = pl.ds(n * 8, 8)
            v_copies.append(copy(number, pksend.at[part], pkrecv.at[side, part], (dx,) + region))
            number += 1
        if region != (0, 0):
            part = pl.ds((first - 24) * 8, count * 8)
            v_copies.append(
                copy(number, vsend.at[part], vmain.at[pl.ds(first * 8, count * 8)], (0,) + region)
            )
            number += 1

    def split_main(low, high):
        for t in range(low, high):
            rows = pl.ds(t * 16, 16)
            value = vmain[rows, :]
            high_part = value.astype(bf16)
            va[rows, pl.ds(0, 128)] = high_part
            vb[rows, pl.ds(0, 128)] = high_part
            va[rows, pl.ds(128, 128)] = (value - high_part.astype(f32)).astype(bf16)

    vmain[tile_rows(47), :] = jnp.zeros((8, 128), f32)
    split_main(0, 12)

    @pl.loop(0, PAIRS)
    def _(p):
        lanes = pl.ds(pl.multiple_of(p * 256, 256), 256)
        w_high = weights[pl.ds(0, 128), lanes]
        tmain[p] = jnp.dot(va[pl.ds(0, 192), :], jnp.concatenate([w_high, w_high], axis=0), preferred_element_type=f32)

    waited = len(started) - len(v_copies)
    for made in started[:waited]:
        made.wait_send()
    for made in v_copies:
        made.wait_recv()
    split_main(12, 24)
    beyond = {}
    for n, region in enumerate(region_list):
        first, count = regions[region]
        merged = jnp.where(outer_low, pkrecv[1, tile_rows(n), :], pkrecv[0, tile_rows(n), :])
        for g in range(0, count, GROUP):
            value = merged if g == 0 else pltpu.roll(merged, (-3 * g) % 128, 1)
            high_part = value.astype(bf16).astype(f32)
            low_part = pltpu.roll(value - high_part, 40, 1)
            value = jnp.where(lane < 40, high_part, jnp.where(lane < 80, low_part, pltpu.roll(high_part, 80, 1)))
            for k in range(g, min(g + GROUP, count)):
                beyond[first + k] = pltpu.roll(value, (-3 * (k - g)) % 128, 1) if k > g else value
    beyond[47] = jnp.zeros((8, 128), f32)
    for t in range(ROWS // 16):
        vb[pl.ds(t * 16, 16), pl.ds(128, 128)] = jnp.concatenate([beyond[2 * t], beyond[2 * t + 1]], axis=0).astype(bf16)

    @pl.loop(0, PAIRS, unroll=UNROLL)
    def _(p):
        pair_lanes = pl.ds(pl.multiple_of(p * 256, 256), 256)
        w_high = weights[pl.ds(0, 128), pair_lanes]
        w_rest = weights[pl.ds(128, 256), pair_lanes]
        t_main = tmain[p] + jnp.dot(vb[pl.ds(0, 192), :], w_rest, preferred_element_type=f32)
        t_out = jnp.dot(
            va[pl.ds(192, 192), :], jnp.concatenate([w_high, w_high], axis=0), preferred_element_type=f32
        ) + jnp.dot(vb[pl.ds(192, 192), :], w_rest, preferred_element_type=f32)
        for j in range(2):
            b = 2 * p + j
            lanes = pl.ds(pl.multiple_of(p * 256 + j * 128, 128), 128)
            block = pl.ds(b, 1)

            def tile(t):
                source, at = (t_main, t) if t < 24 else (t_out, t - 24)
                return source[at * 8 : at * 8 + 8, j * 128 : (j + 1) * 128]

            def u(t):
                return spread_weights[b, tile_rows(t), :]

            p42 = tile(42) * u(14)
            p43 = tile(43) * u(15)
            p445 = tile(44) * u(16) + tile(45) * u(17)
            p46 = tile(46) * u(18)
            alive = lax.broadcasted_iota(jnp.int32, (1, 128), 1) < counts[b]
            pushes = []
            rows = []
            for c in range(3):
                acc = jnp.where((sub >> 1) == c, p445, 0.0) + jnp.where(sub == c, p46, 0.0)
                if c < 2:
                    acc = acc + jnp.where((sub >> 2) == c, p42, 0.0)
                else:
                    acc = acc + p43
                other = tile(c * 8) * u(0)
                for z in range(1, 8):
                    other = other + tile(c * 8 + z) * u(z)
                acc = acc + tile(24 + c * 2) * u(8) + tile(25 + c * 2) * u(9) + tile(30 + c) * u(10)
                acc = acc + tile(33 + c * 2) * u(11) + tile(34 + c * 2) * u(12) + tile(39 + c) * u(13)
                sampled = jnp.sum(acc + other, axis=0, keepdims=True)
                speed = drop_vel[c, block, :]
                moved = speed + relax * (sampled - speed)
                pushes.append(jnp.where(alive, couple * (moved - sampled), 0.0))
                rows.append(jnp.where(alive, moved, 0.0))
            for c in range(3):
                rows.append(jnp.where(alive, drop_frac[c, block, :], 0.0) + rows[c])
            block_state = jnp.zeros((8, 128), f32)
            for c in range(6):
                block_state = jnp.where(sub == c, rows[c], block_state)
            states[pl.ds(pl.multiple_of(b * 8, 8), 8), :] = block_state

            by_half = jnp.where((sub >> 1) == 0, pushes[0], jnp.where((sub >> 1) == 1, pushes[1], pushes[2]))
            by_row = jnp.where(sub == 0, pushes[0], jnp.where(sub == 1, pushes[1], pushes[2]))
            by_four = jnp.where(sub < 4, pushes[0], pushes[1])
            plan = [(pushes[c], z) for c in range(3) for z in range(8)]
            plan += [(pushes[c], 8 + k) for c in range(3) for k in range(2)]
            plan += [(pushes[c], 10) for c in range(3)]
            plan += [(pushes[c], 11 + k) for c in range(3) for k in range(2)]
            plan += [(pushes[c], 13) for c in range(3)]
            plan += [(by_four, 14), (pushes[2], 15), (by_half, 16), (by_half, 17), (by_row, 18)]
            sources = [push * u(t) for push, t in plan] + [jnp.zeros((8, 128), f32)]
            for t in range(ROWS // 16):
                value = jnp.concatenate([sources[2 * t], sources[2 * t + 1]], axis=0)
                high_part = value.astype(bf16)
                shi[pl.ds(t * 16, 16), lanes] = high_part
                slo[pl.ds(t * 16, 16), lanes] = (value - high_part.astype(f32)).astype(bf16)

    codes = [dest[b] for b in range(BLOCKS)]
    wide = lax.broadcasted_iota(jnp.int32, (8, 128), 1)
    owner = wide >> 3
    code = jnp.zeros((8, 128), jnp.int32)
    for b in range(BLOCKS):
        code = jnp.where(owner == b, codes[b], code)
    rank = jnp.zeros((8, 128), jnp.int32)
    for b in range(BLOCKS):
        rank = rank + jnp.where((code == codes[b]) & (owner > b), 1, 0)
    lanes_of = jnp.where(code < 13, code, code - 1) * 2 + rank
    key = jnp.where(code == 13, -1, lanes_of * 8 + (wide & 7))[0:1, :]
    value = states[...]
    part_0 = value.astype(bf16)
    value = value - part_0.astype(f32)
    part_1 = value.astype(bf16)
    part_2 = (value - part_1.astype(f32)).astype(bf16)
    chosen = jnp.where(lax.broadcasted_iota(jnp.int32, (416, 128), 0) == key, 1.0, 0.0).astype(bf16)
    outbox[...] = (
        jnp.dot(chosen, part_0, preferred_element_type=f32)
        + jnp.dot(chosen, part_1, preferred_element_type=f32)
        + jnp.dot(chosen, part_2, preferred_element_type=f32)
    )
    def over_droplets(source, weight):
        return lax.dot_general(source, weight, (((1,), (1,)), ((), ())), preferred_element_type=f32)

    near = over_droplets(shi[...], weights[pl.ds(0, 256), :])
    last = over_droplets(slo[...], jnp.concatenate([weights[pl.ds(0, 128), :], weights[pl.ds(256, 128), :]], axis=0))
    f_main[...] = near[:, 0:128] + near[:, 128:256] + last[:, 0:128]
    part_high = over_droplets(shi[...], weights[pl.ds(256, 128), :])
    f_beyond[...] = part_high + last[:, 128:256]
    shifted = lane - 80
    spot = jnp.where(lane < 36, third, jnp.where((lane >= 80) & (lane < 116), (shifted * 171) >> 9, -1))

    f_copies = []
    for n, region in enumerate(region_list):
        first, count = regions[region]
        packed = None
        for g in range(0, count, GROUP):
            value = jnp.zeros((8, 128), f32)
            for k in range(g, min(g + GROUP, count)):
                rows = tile_rows(first + k)
                if region != (0, 0):
                    fsend[tile_rows(first - 24 + k), :] = f_main[rows, :]
                both = f_beyond[rows, :]
                value = jnp.where(spot == k - g, pltpu.roll(both, 3 * (k - g), 1) if k > g else both, value)
            value = value + pltpu.roll(value, 48, 1)
            packed = value if g == 0 else jnp.where(lane < 3 * g, packed, pltpu.roll(value, 3 * g, 1))
        fpsend[tile_rows(n), :] = packed
        back = (-region[0], -region[1])
        for side, dx in ((0, -1), (1, 1)):
            part = pl.ds(n * 8, 8)
            f_copies.append(copy(number, fpsend.at[part], fprecv.at[side, part], (-dx,) + back))
            number += 1
        if region != (0, 0):
            part = pl.ds((first - 24) * 8, count * 8)
            f_copies.append(copy(number, fsend.at[part], frecv.at[part], (0,) + back))
            number += 1

    h_copies = []
    for d in far_first:
        part = pl.ds(all_dirs.index(d) * 16, 16)
        h_copies.append(copy(number, outbox.at[part], inbox.at[part], d))
        number += 1

    stay_rows = lax.broadcasted_iota(jnp.int32, (16, 128), 0)
    stays = jnp.zeros((16, 128), jnp.int32)
    for b in range(BLOCKS):
        stays = jnp.where(stay_rows == b, codes[b], stays)
    for c in range(6):
        arrived[c, pl.ds(0, 16), :] = jnp.where(stays == 13, states[pl.ds(c, 16, stride=8), :], 0.0)

    for made in started[waited : waited + len(v_copies)]:
        made.wait_send()
    for made in f_copies:
        made.wait_recv()
    for n, region in enumerate(region_list):
        first, count = regions[region]
        merged = jnp.where(outer_low, fprecv[1, tile_rows(n), :], fprecv[0, tile_rows(n), :])
        for k in range(count):
            value = jnp.where((lane < 2) | (lane == 127), pltpu.roll(merged, (127 - 3 * k) % 128, 1), 0.0)
            rows = tile_rows(first + k)
            if region == (0, 0):
                f_main[rows, :] += value
            else:
                vmain[rows, :] = frecv[tile_rows(first - 24 + k), :] + value

    def row_of(t, r):
        return vmain[pl.ds(t * 8 + r, 1), :]

    def corner_row(region, c, y, z):
        return row_of(regions[region][0], corner_rows(region).index((c, y, z)))

    for c in range(3):
        for z in range(8):
            total = f_main[tile_rows(c * 8 + z), :]
            lines = [row_of(24 + c * 2, z), row_of(25 + c * 2, z), row_of(30 + c, z)]
            if z < 2 or z == 7:
                if z < 2:
                    total = total + vmain[tile_rows(33 + c * 2 + z), :]
                    low, high = (-1, -1), (1, -1)
                else:
                    total = total + vmain[tile_rows(39 + c), :]
                    low, high = (-1, 1), (1, 1)
                lines[0] = lines[0] + corner_row(low, c, 0, z)
                lines[1] = lines[1] + corner_row(low, c, 1, z)
                lines[2] = lines[2] + corner_row(high, c, 7, z)
            beside = jnp.where(sub == 0, lines[0], jnp.where(sub == 1, lines[1], jnp.where(sub == 7, lines[2], 0.0)))
            force[c, tile_rows(z), :] = total + beside

    for made in h_copies:
        made.wait_recv()
    for c in range(6):
        arrived[c, pl.ds(16, 52), :] = inbox[pl.ds(c, 52, stride=8), :]
    for made in started[waited + len(v_copies) :]:
        made.wait_send()


def deliver(state, force, arrived, state_hbm, force_hbm, arrived_hbm, sem):
    copies = [
        pltpu.make_async_copy(src, dst, sem.at[n])
        for n, (src, dst) in enumerate(((state, state_hbm), (force, force_hbm), (arrived, arrived_hbm)))
    ]
    for made in copies:
        made.start()
    for made in copies:
        made.wait()


def solution(mesh):
    sizes = tuple(mesh.shape[a] for a in ("gx", "gy", "gz"))

    def body(*refs):
        kernel(sizes, *refs)

    def local(pops, coarse_pops, interface, drop_vel, drop_frac, home, counts, dest):
        vmem = pl.BlockSpec(memory_space=pltpu.VMEM)
        anywhere = pl.BlockSpec(memory_space=pl.ANY)
        made = pl.pallas_call(
            body,
            out_shape=(
                pltpu.VMEM((19, 64, 128), f32),
                pltpu.VMEM((3, 64, 128), f32),
                pltpu.VMEM((6, 68, 128), f32),
            ),
            in_specs=[pl.BlockSpec(memory_space=pltpu.HBM)] * 8,
            out_specs=(vmem, vmem, vmem),
            scratch_shapes=[
                pltpu.VMEM((19, 64, 128), f32),
                pltpu.VMEM((19, 8, 8, 128), bf16),
                pltpu.VMEM((8, 8, 128), jnp.int32),
                pltpu.VMEM((3, 16, 128), f32),
                pltpu.VMEM((3, 16, 128), f32),
                pltpu.VMEM((16, 128), jnp.int32),
                pltpu.SMEM((BLOCKS,), jnp.int32),
                pltpu.SMEM((BLOCKS,), jnp.int32),
                pltpu.VMEM((19, 64, 128), f32),
                pltpu.VMEM((19, 64, 128), f32),
                pltpu.VMEM((2, POST_TILES * 8, 128), f32),
                pltpu.VMEM((2, POST_TILES * 8, 128), f32),
                pltpu.VMEM((ROWS, 128), f32),
                pltpu.VMEM((24 * 8, 128), f32),
                pltpu.VMEM((72, 128), f32),
                pltpu.VMEM((2, 72, 128), f32),
                pltpu.VMEM((ROWS, 256), bf16),
                pltpu.VMEM((ROWS, 256), bf16),
                pltpu.VMEM((384, WIDE), bf16),
                pltpu.VMEM((12, 16, 128), f32),
                pltpu.VMEM((3, 16, 128), jnp.int32),
                pltpu.VMEM((BLOCKS, U_TILES * 8, 128), f32),
                pltpu.VMEM((PAIRS, 192, 256), f32),
                pltpu.VMEM((ROWS, WIDE), bf16),
                pltpu.VMEM((ROWS, WIDE), bf16),
                pltpu.VMEM((ROWS, 128), f32),
                pltpu.VMEM((ROWS, 128), f32),
                pltpu.VMEM((24 * 8, 128), f32),
                pltpu.VMEM((24 * 8, 128), f32),
                pltpu.VMEM((72, 128), f32),
                pltpu.VMEM((2, 72, 128), f32),
                pltpu.VMEM((BLOCKS * 8, 128), f32),
                pltpu.VMEM((416, 128), f32),
                pltpu.VMEM((416, 128), f32),
                pltpu.SemaphoreType.DMA((N_MSG,)),
                pltpu.SemaphoreType.DMA((N_MSG,)),
                pltpu.SemaphoreType.DMA((8,)),
            ],
            compiler_params=pltpu.CompilerParams(
                collective_id=0, has_side_effects=True, vmem_limit_bytes=36 * 1024 * 1024
            ),
            name="channel",
        )(
            *(
                pltpu.with_memory_space_constraint(x, pltpu.HBM)
                for x in (pops.reshape(19, 64, 128), coarse_pops, interface, drop_vel, drop_frac, home, counts, dest)
            )
        )
        state, force, arrived = pl.pallas_call(
            deliver,
            out_shape=(
                jax.ShapeDtypeStruct((19, 64, 128), f32),
                jax.ShapeDtypeStruct((3, 64, 128), f32),
                jax.ShapeDtypeStruct((6, 68, 128), f32),
            ),
            in_specs=[vmem] * 3,
            out_specs=(anywhere,) * 3,
            scratch_shapes=[pltpu.SemaphoreType.DMA((3,))],
            compiler_params=pltpu.CompilerParams(vmem_limit_bytes=8 * 1024 * 1024),
            name="deliver",
        )(*made)
        return state.reshape(19, 8, 8, 128), force.reshape(3, 8, 8, 128), arrived

    return jax.shard_map(
        local,
        mesh=mesh,
        in_specs=(
            P(None, "gz", "gy", "gx"),
            P(None, "gz", "gy", "gx"),
            P("gz", "gy", "gx"),
            P(None, ("gx", "gy", "gz"), None),
            P(None, ("gx", "gy", "gz"), None),
            P(("gx", "gy", "gz"), None),
            P(("gx", "gy", "gz")),
            P(("gx", "gy", "gz")),
        ),
        out_specs=(
            P(None, "gz", "gy", "gx"),
            P(None, "gz", "gy", "gx"),
            P(None, ("gx", "gy", "gz"), None),
        ),
        check_vma=False,
    )
```

```python
import math

import jax
import jax.numpy as jnp
import numpy as np
from jax import lax
from jax.experimental import pallas as pl
from jax.experimental.pallas import tpu as pltpu
from jax.sharding import PartitionSpec as P

lattice = [
    (0, 0, 0), (1, 0, 0), (-1, 0, 0), (0, 1, 0), (0, -1, 0), (0, 0, 1), (0, 0, -1),
    (1, 1, 0), (-1, -1, 0), (1, -1, 0), (-1, 1, 0), (1, 0, 1), (-1, 0, -1), (1, 0, -1),
    (-1, 0, 1), (0, 1, 1), (0, -1, -1), (0, 1, -1), (0, -1, 1),
]
weights_table = [1.0 / 3.0] + [1.0 / 18.0] * 6 + [1.0 / 36.0] * 12
opposite = [0, 2, 1, 4, 3, 6, 5, 8, 7, 10, 9, 12, 11, 14, 13, 16, 15, 18, 17]
inverse_tau = 0.8
relax = 0.5
couple = 8.0
f32 = jnp.float32
bf16 = jnp.bfloat16

face_pops = {}
for axis in range(3):
    for sign in (1, -1):
        d = [0, 0, 0]
        d[axis] = sign
        face_pops[tuple(d)] = [i for i in range(19) if lattice[i][axis] == sign]
post_msgs = {}
tiles = 0
for i in list(range(7, 19)) + [3, 4, 5, 6, 1, 2]:
    c = lattice[i]
    count = 1 if (abs(c[0]) + abs(c[1]) + abs(c[2]) > 1 or c[0] != 0) else 5
    post_msgs[c] = (tiles, count)
    tiles += count
POST_TILES = tiles

regions = {
    (0, 0): (0, 24),
    (-1, 0): (24, 6),
    (1, 0): (30, 3),
    (0, -1): (33, 6),
    (0, 1): (39, 3),
    (-1, -1): (42, 2),
    (1, -1): (44, 1),
    (-1, 1): (45, 1),
    (1, 1): (46, 1),
}
region_list = list(regions)[::-1]
ROWS = 48 * 8
all_dirs = [(x, y, z) for z in (-1, 0, 1) for y in (-1, 0, 1) for x in (-1, 0, 1) if (x, y, z) != (0, 0, 0)]
far_first = sorted(all_dirs, key=lambda d: -abs(d[0]) - abs(d[1]) - abs(d[2]))
near_dirs = [d for d in far_first if 0 in d]
U_TILES = 19
WIDE = 2048
N_POST = 18
N_MSG = 2 * N_POST + 3 * 26
PAIRS = 8
BLOCKS = 16
UNROLL = 4
GROUP = 12


def corner_rows(region):
    dy, dz = region
    ys = [7] if dy == 1 else [0, 1]
    zs = [7] if dz == 1 else [0, 1]
    return [(c, y, z) for c in range(3) for z in zs for y in ys]


def tile_rows(t):
    return pl.ds(t * 8, 8)


def kernel(
    sizes,
    pops_hbm, coarse_hbm, interface_hbm, drop_vel_hbm, drop_frac_hbm, home_hbm, counts_hbm, dest_hbm,
    state_out, force, arrived,
    pops, coarse, interface, drop_vel, drop_frac, home, counts, dest,
    posts, state_mid, psend, precv, vmain, vsend, pksend, pkrecv, va, vb, weights,
    taps, homes, spread_weights, tmain, partial, shi, slo, f_main, f_beyond, fsend, frecv, fpsend, fprecv, states, outbox, inbox,
    send_sem, recv_sem, in_sem,
):
    n_x, n_y, n_z = sizes
    me = (lax.axis_index("gx"), lax.axis_index("gy"), lax.axis_index("gz"))
    level = me[2]
    at_bottom = level == 0
    at_top = level == n_z - 1

    def moved_by(axis, step, size):
        if step == 0:
            return me[axis]
        return lax.rem(me[axis] + (step + size), size)

    coords = {
        (axis, step): moved_by(axis, step, size)
        for axis, size in enumerate(sizes)
        for step in (-1, 0, 1)
    }

    def device(d):
        return {"gx": coords[0, d[0]], "gy": coords[1, d[1]], "gz": coords[2, d[2]]}

    lane = lax.broadcasted_iota(jnp.int32, (8, 128), 1)
    sub = lax.broadcasted_iota(jnp.int32, (8, 128), 0)

    third = (lane * 171) >> 9
    outer_low = lane - third * 3 == 0
    started = []

    def copy(index, src, dst, d):
        made = pltpu.make_async_remote_copy(
            src_ref=src,
            dst_ref=dst,
            send_sem=send_sem.at[index],
            recv_sem=recv_sem.at[index],
            device_id=device(d),
            device_id_type=pl.DeviceIdType.MESH,
        )
        made.start()
        started.append(made)
        return made

    barrier = pltpu.get_barrier_semaphore()
    for d in near_dirs:
        pl.semaphore_signal(barrier, inc=1, device_id=device(d), device_id_type=pl.DeviceIdType.MESH)

    loads = []
    for n, (src, dst) in enumerate(
        (
            (pops_hbm, pops),
            (coarse_hbm, coarse),
            (interface_hbm, interface),
            (drop_vel_hbm, drop_vel),
            (drop_frac_hbm, drop_frac),
            (home_hbm, home),
            (counts_hbm, counts),
            (dest_hbm, dest),
        )
    ):
        loads.append(pltpu.make_async_copy(src, dst, in_sem.at[n]))
        loads[-1].start()
    def macroscopic(values):
        plus = {i: values[i] + values[i + 1] for i in range(1, 19, 2)}
        minus = {i: values[i] - values[i + 1] for i in range(1, 19, 2)}
        axes = plus[1] + plus[3] + plus[5]
        edges = (plus[7] + plus[9]) + (plus[11] + plus[13]) + (plus[15] + plus[17])
        density = values[0] * weights_table[0] + axes * weights_table[1] + edges * weights_table[7]
        inverse = 1.0 / density
        near, far = weights_table[1] * inverse, weights_table[7] * inverse
        flow = [
            minus[1] * near + ((minus[7] + minus[9]) + (minus[11] + minus[13])) * far,
            minus[3] * near + ((minus[7] - minus[9]) + (minus[15] + minus[17])) * far,
            minus[5] * near + ((minus[11] - minus[13]) + (minus[15] - minus[17])) * far,
        ]
        return density, flow

    def collide(source):
        @pl.loop(0, 8, unroll=2)
        def _(z):
            rows = pl.ds(pl.multiple_of(z * 8, 8), 8)
            values = [source[i, rows, :] for i in range(19)]
            density, flow = macroscopic(values)
            square = flow[0] * flow[0] + flow[1] * flow[1] + flow[2] * flow[2]
            inside = interface[z] == 1
            scaled = density * inverse_tau
            base = scaled - square * (1.5 * scaled)
            first, second = scaled * 3.0, scaled * 4.5

            def put(i, balance):
                relaxed = values[i] * (1.0 - inverse_tau) + balance
                posts[i, rows, :] = jnp.where(inside, coarse[i, z].astype(f32), relaxed)

            put(0, base)
            for i in range(1, 19, 2):
                along = None
                for axis in range(3):
                    sign = lattice[i][axis]
                    if sign == 1:
                        along = flow[axis] if along is None else along + flow[axis]
                    if sign == -1:
                        along = along - flow[axis]
                even = base + along * along * second
                odd = along * first
                put(i, even + odd)
                put(i + 1, even - odd)

    def pack_posts(r):
        for number, (d, (first, count)) in enumerate(post_msgs.items()):
            layer = {a: (7 if d[a] == 1 else 0) for a in (1, 2)}
            if d in face_pops:
                listed = face_pops[d]
            else:
                listed = [lattice.index(d)]
            if d[0] != 0 and d[1] == 0 and d[2] == 0:
                acc = jnp.zeros((8, 128), f32)
                from_lane = 127 if d[0] == 1 else 0
                for k, i in enumerate(listed):
                    for z in range(8):
                        spot = k * 8 + z
                        turned = pltpu.roll(posts[i, tile_rows(z), :], (spot - from_lane) % 128, 1)
                        acc = jnp.where(lane == spot, turned, acc)
                psend[r, tile_rows(first), :] = acc
            elif d[2] != 0:
                for k, i in enumerate(listed):
                    psend[r, tile_rows(first + k), :] = posts[i, tile_rows(layer[2]), :]
            else:
                for k, i in enumerate(listed):
                    psend[r, tile_rows(first + k), :] = posts[i, pl.ds(layer[1], 8, stride=8), :]

    def send_posts(r):
        copies = {}
        for number, (d, (first, count)) in enumerate(post_msgs.items()):
            part = pl.ds(first * 8, count * 8)
            copies[d] = copy(r * N_POST + number, psend.at[r, part], precv.at[r, part], d)
        return copies

    def pull(r, i):
        cx, cy, cz = lattice[i]
        far = 127 if cx == 1 else 0

        def halo(d):
            first, count = post_msgs[d]
            k = face_pops[d].index(i) if d in face_pops and d[0] == 0 else 0
            return first + k

        def x_shift(value, beyond):
            return pltpu.roll(jnp.where(lane == far, beyond, value), cx % 128, 1)

        def y_shift(value, row):
            edge = 0 if cy == 1 else 7
            return jnp.where(sub == edge, row, pltpu.roll(value, cy % 8, 0))

        wanted = [z - cz for z in range(8)]
        planes = {z: posts[i, tile_rows(z), :] for z in range(8) if z in wanted}
        outer = None
        if cz != 0:
            outer = precv[r, tile_rows(halo((0, 0, cz))), :]
        if cx != 0:
            packed = precv[r, tile_rows(post_msgs[(cx, 0, 0)][0]), :]
            k = face_pops[(cx, 0, 0)].index(i)
            for z in planes:
                planes[z] = x_shift(planes[z], pltpu.roll(packed, (far - (k * 8 + z)) % 128, 1))
            if cz != 0:
                outer = x_shift(outer, precv[r, tile_rows(halo((cx, 0, cz))), :])
        if cy != 0:
            place = halo((0, cy, 0))
            if cx != 0:
                side = x_shift(precv[r, tile_rows(place), :], precv[r, tile_rows(halo((cx, cy, 0))), :])
                for z in planes:
                    planes[z] = y_shift(planes[z], side[z : z + 1, :])
            else:
                for z in planes:
                    planes[z] = y_shift(planes[z], precv[r, pl.ds(place * 8 + z, 1), :])
            if cz != 0:
                row = halo((0, cy, cz)) * 8 + (7 if cy == 1 else 0)
                outer = y_shift(outer, precv[r, pl.ds(row, 1), :])
        out = [planes[z] if z in planes else outer for z in wanted]
        if cz == 1:
            out[0] = jnp.where(at_bottom, posts[opposite[i], tile_rows(0), :], out[0])
        if cz == -1:
            out[7] = jnp.where(at_top, posts[opposite[i], tile_rows(7), :], out[7])
        return out

    def stream(r, copies, into):
        for made in copies.values():
            made.wait_recv()
        for i in range(19):
            out = pull(r, i)
            for z in range(8):
                into[i, tile_rows(z), :] = out[z]

    def prepare():
        for axis in range(3):
            angle = drop_frac[axis] * (0.5 * math.pi)
            sine = jnp.sin(angle)
            cosine = jnp.cos(angle)
            taps[axis * 4 + 0] = 0.25 - 0.25 * sine
            taps[axis * 4 + 1] = 0.25 + 0.25 * cosine
            taps[axis * 4 + 2] = 0.25 + 0.25 * sine
            taps[axis * 4 + 3] = 0.25 - 0.25 * cosine
        cells = home[...]
        homes[0] = (cells & 127) - 1
        homes[1] = ((cells >> 7) & 7) - 1
        homes[2] = (cells >> 10) - 1

    def picked(offset, weight):
        zero = jnp.zeros(offset.shape, f32)
        return jnp.where(
            offset == 0,
            weight[0],
            jnp.where(offset == 1, weight[1], jnp.where(offset == 2, weight[2], jnp.where(offset == 3, weight[3], zero))),
        )

    rows16 = lax.broadcasted_iota(jnp.int32, (16, 128), 0)

    def build_x_weights():
        @pl.loop(0, BLOCKS)
        def _(b):
            block = pl.ds(b, 1)
            lanes = pl.ds(pl.multiple_of(b * 128, 128), 128)
            first = homes[0, block, :]
            weight = [taps[k, block, :] for k in range(4)]
            for t in range(8):
                value = picked(rows16 + t * 16 - first, weight)
                high_part = value.astype(bf16)
                weights[pl.ds(t * 16, 16), lanes] = high_part
                weights[pl.ds(128 + t * 16, 16), lanes] = (value - high_part.astype(f32)).astype(bf16)
            def outside(at):
                row = rows16 - at
                cell = jnp.where(row == 0, -1, jnp.where(row == 1, 128, jnp.where(row == 2, 129, -1000)))
                return picked(cell - first, weight)

            value = outside(0)
            high_part = value.astype(bf16)
            weights[pl.ds(256, 16), lanes] = high_part
            weights[pl.ds(272, 16), lanes] = jnp.zeros((16, 128), bf16)
            weights[pl.ds(288, 16), lanes] = outside(8).astype(bf16)
            weights[pl.ds(304, 32), lanes] = jnp.zeros((32, 128), bf16)
            weights[pl.ds(336, 16), lanes] = (value - high_part.astype(f32)).astype(bf16)
            weights[pl.ds(352, 32), lanes] = jnp.zeros((32, 128), bf16)

    def build_yz_weights():
        @pl.loop(0, BLOCKS)
        def _(b):
            block = pl.ds(b, 1)
            hy = homes[1, block, :]
            hz = homes[2, block, :]
            wy = [taps[4 + k, block, :] for k in range(4)]
            wz = [taps[8 + k, block, :] for k in range(4)]
            y_main = picked(sub - hy, wy)
            z_main = picked(sub - hz, wz)
            y_out = [picked(y - hy, wy) for y in (8, 9, -1)]
            z_out = [picked(z - hz, wz) for z in (8, 9, -1)]
            z_out = [jnp.where(at_top, 0.0, z_out[0]), jnp.where(at_top, 0.0, z_out[1]), jnp.where(at_bottom, 0.0, z_out[2])]
            even = (sub & 1) == 0
            y_pair = jnp.where(even, y_out[0], y_out[1])
            z_pair = jnp.where(even, z_out[0], z_out[1])
            both = y_pair * jnp.where((sub & 2) == 0, z_out[0], z_out[1])
            made = [y_main * z_main[z : z + 1, :] for z in range(8)]
            made += [z_main * y_out[k] for k in range(3)]
            made += [y_main * z_out[k] for k in range(3)]
            made.append(both)
            made.append(jnp.where(sub < 4, both, 0.0))
            made.append(jnp.where(sub < 6, y_out[2] * z_pair, 0.0))
            made.append(jnp.where(sub < 6, y_pair * z_out[2], 0.0))
            made.append(jnp.where(sub < 3, y_out[2] * z_out[2], 0.0))
            for t in range(U_TILES):
                spread_weights[b, tile_rows(t), :] = made[t]

    for made in loads[:3]:
        made.wait()
    collide(pops)
    pack_posts(0)
    pl.semaphore_wait(barrier, len(near_dirs))
    first_copies = send_posts(0)
    stream(0, first_copies, state_mid)
    collide(state_mid)
    pack_posts(1)
    second_copies = send_posts(1)
    for made in loads[3:]:
        made.wait()
    prepare()
    build_x_weights()
    build_yz_weights()
    stream(1, second_copies, state_out)

    for z in range(8):
        values = [state_out[i, tile_rows(z), :] for i in range(19)]
        flow = macroscopic(values)[1]
        for c in range(3):
            vmain[tile_rows(c * 8 + z), :] = flow[c]

    def sent_tile(region, k):
        dy, dz = region
        if region == (0, 0):
            return vmain[tile_rows(k), :]
        if dz == 0:
            start = (k // 2) * 64 + k % 2 if dy == -1 else k * 64 + 7
            return vmain[pl.ds(start, 8, stride=8), :]
        if dy == 0:
            tile = (k // 2) * 8 + k % 2 if dz == -1 else k * 8 + 7
            return vmain[tile_rows(tile), :]
        acc = jnp.zeros((8, 128), f32)
        for r, (c, y, z) in enumerate(corner_rows(region)[k * 8 : k * 8 + 8]):
            acc = jnp.where(sub == r, vmain[pl.ds(c * 64 + z * 8 + y, 1), :], acc)
        return acc

    v_copies = []
    v_near = []
    number = 2 * N_POST
    for n, region in enumerate(region_list):
        first, count = regions[region]
        packed = jnp.zeros((8, 128), f32)
        for k in range(count):
            value = sent_tile(region, k)
            if region != (0, 0):
                vsend[tile_rows(first - 24 + k), :] = value
            packed = jnp.where(third == k, pltpu.roll(value, 3 * k + 1, 1), packed)
        pksend[tile_rows(n), :] = packed
        for side, dx in ((0, -1), (1, 1)):
            part = pl.ds(n * 8, 8)
            made = copy(number, pksend.at[part], pkrecv.at[side, part], (dx,) + region)
            (v_near if region == (0, 0) else v_copies).append(made)
            number += 1
        if region != (0, 0):
            part = pl.ds((first - 24) * 8, count * 8)
            made = copy(number, vsend.at[part], vmain.at[pl.ds(first * 8, count * 8)], (0,) + region)
            (v_near if 0 in region else v_copies).append(made)
            number += 1

    def split_main(low, high):
        for t in range(low, high):
            rows = pl.ds(t * 16, 16)
            value = vmain[rows, :]
            high_part = value.astype(bf16)
            va[rows, pl.ds(0, 128)] = high_part
            vb[rows, pl.ds(0, 128)] = high_part
            va[rows, pl.ds(128, 128)] = (value - high_part.astype(f32)).astype(bf16)

    vmain[tile_rows(47), :] = jnp.zeros((8, 128), f32)
    split_main(0, 12)

    @pl.loop(0, PAIRS)
    def _(p):
        lanes = pl.ds(pl.multiple_of(p * 256, 256), 256)
        w_high = weights[pl.ds(0, 128), lanes]
        tmain[p] = jnp.dot(va[pl.ds(0, 192), :], jnp.concatenate([w_high, w_high], axis=0), preferred_element_type=f32)

    waited = 2 * N_POST
    for made in started[:waited]:
        made.wait_send()
    def unpack(n, region):
        first, count = regions[region]
        merged = jnp.where(outer_low, pkrecv[1, tile_rows(n), :], pkrecv[0, tile_rows(n), :])
        for g in range(0, count, GROUP):
            value = merged if g == 0 else pltpu.roll(merged, (-3 * g) % 128, 1)
            high_part = value.astype(bf16).astype(f32)
            low_part = pltpu.roll(value - high_part, 40, 1)
            value = jnp.where(lane < 40, high_part, jnp.where(lane < 80, low_part, pltpu.roll(high_part, 80, 1)))
            for k in range(g, min(g + GROUP, count)):
                beyond[first + k] = pltpu.roll(value, (-3 * (k - g)) % 128, 1) if k > g else value

    def store_beyond(low, high):
        for t in range(low, high):
            vb[pl.ds(t * 16, 16), pl.ds(128, 128)] = jnp.concatenate([beyond[2 * t], beyond[2 * t + 1]], axis=0).astype(bf16)

    beyond = {47: jnp.zeros((8, 128), f32)}
    for made in v_near:
        made.wait_recv()
    split_main(12, 21)
    unpack(region_list.index((0, 0)), (0, 0))
    store_beyond(0, 12)

    @pl.loop(0, PAIRS, unroll=UNROLL)
    def _(p):
        pair_lanes = pl.ds(pl.multiple_of(p * 256, 256), 256)
        w_high = weights[pl.ds(0, 128), pair_lanes]
        t_main = tmain[p] + jnp.dot(
            vb[pl.ds(0, 192), :], weights[pl.ds(128, 256), pair_lanes], preferred_element_type=f32
        )
        t_face = jnp.dot(
            va[pl.ds(192, 144), :], jnp.concatenate([w_high, w_high], axis=0), preferred_element_type=f32
        ) + jnp.dot(
            vb[pl.ds(192, 144), pl.ds(0, 128)], weights[pl.ds(128, 128), pair_lanes], preferred_element_type=f32
        )
        for j in range(2):
            b = 2 * p + j

            def tile(t):
                source, at = (t_main, t) if t < 24 else (t_face, t - 24)
                return source[at * 8 : at * 8 + 8, j * 128 : (j + 1) * 128]

            def u(t):
                return spread_weights[b, tile_rows(t), :]

            for c in range(3):
                acc = tile(24 + c * 2) * u(8) + tile(25 + c * 2) * u(9) + tile(30 + c) * u(10)
                acc = acc + tile(33 + c * 2) * u(11) + tile(34 + c * 2) * u(12) + tile(39 + c) * u(13)
                other = tile(c * 8) * u(0)
                for z in range(1, 8):
                    other = other + tile(c * 8 + z) * u(z)
                partial[b, tile_rows(c), :] = acc + other

    for made in v_copies:
        made.wait_recv()
    split_main(21, 24)
    for n, region in enumerate(region_list):
        if region != (0, 0):
            unpack(n, region)
    store_beyond(12, 24)

    @pl.loop(0, PAIRS, unroll=UNROLL)
    def _(p):
        pair_lanes = pl.ds(pl.multiple_of(p * 256, 256), 256)
        w_high = weights[pl.ds(0, 128), pair_lanes]
        t_side = jnp.dot(
            vb[pl.ds(192, 144), pl.ds(128, 128)], weights[pl.ds(256, 128), pair_lanes], preferred_element_type=f32
        )
        t_corner = jnp.dot(
            va[pl.ds(336, 48), :], jnp.concatenate([w_high, w_high], axis=0), preferred_element_type=f32
        ) + jnp.dot(vb[pl.ds(336, 48), :], weights[pl.ds(128, 256), pair_lanes], preferred_element_type=f32)
        for j in range(2):
            b = 2 * p + j
            lanes = pl.ds(pl.multiple_of(p * 256 + j * 128, 128), 128)
            block = pl.ds(b, 1)

            def tile(t):
                source, at = (t_side, t - 24) if t < 42 else (t_corner, t - 42)
                return source[at * 8 : at * 8 + 8, j * 128 : (j + 1) * 128]

            def u(t):
                return spread_weights[b, tile_rows(t), :]

            p42 = tile(42) * u(14)
            p43 = tile(43) * u(15)
            p445 = tile(44) * u(16) + tile(45) * u(17)
            p46 = tile(46) * u(18)
            alive = lax.broadcasted_iota(jnp.int32, (1, 128), 1) < counts[b]
            pushes = []
            rows = []
            for c in range(3):
                acc = jnp.where((sub >> 1) == c, p445, 0.0) + jnp.where(sub == c, p46, 0.0)
                if c < 2:
                    acc = acc + jnp.where((sub >> 2) == c, p42, 0.0)
                else:
                    acc = acc + p43
                other = partial[b, tile_rows(c), :]
                acc = acc + tile(24 + c * 2) * u(8) + tile(25 + c * 2) * u(9) + tile(30 + c) * u(10)
                acc = acc + tile(33 + c * 2) * u(11) + tile(34 + c * 2) * u(12) + tile(39 + c) * u(13)
                sampled = jnp.sum(acc + other, axis=0, keepdims=True)
                speed = drop_vel[c, block, :]
                moved = speed + relax * (sampled - speed)
                pushes.append(jnp.where(alive, couple * (moved - sampled), 0.0))
                rows.append(jnp.where(alive, moved, 0.0))
            for c in range(3):
                rows.append(jnp.where(alive, drop_frac[c, block, :], 0.0) + rows[c])
            block_state = jnp.zeros((8, 128), f32)
            for c in range(6):
                block_state = jnp.where(sub == c, rows[c], block_state)
            states[pl.ds(pl.multiple_of(b * 8, 8), 8), :] = block_state

            by_half = jnp.where((sub >> 1) == 0, pushes[0], jnp.where((sub >> 1) == 1, pushes[1], pushes[2]))
            by_row = jnp.where(sub == 0, pushes[0], jnp.where(sub == 1, pushes[1], pushes[2]))
            by_four = jnp.where(sub < 4, pushes[0], pushes[1])
            plan = [(pushes[c], z) for c in range(3) for z in range(8)]
            plan += [(pushes[c], 8 + k) for c in range(3) for k in range(2)]
            plan += [(pushes[c], 10) for c in range(3)]
            plan += [(pushes[c], 11 + k) for c in range(3) for k in range(2)]
            plan += [(pushes[c], 13) for c in range(3)]
            plan += [(by_four, 14), (pushes[2], 15), (by_half, 16), (by_half, 17), (by_row, 18)]
            sources = [push * u(t) for push, t in plan] + [jnp.zeros((8, 128), f32)]
            for t in range(ROWS // 16):
                value = jnp.concatenate([sources[2 * t], sources[2 * t + 1]], axis=0)
                high_part = value.astype(bf16)
                shi[pl.ds(t * 16, 16), lanes] = high_part
                slo[pl.ds(t * 16, 16), lanes] = (value - high_part.astype(f32)).astype(bf16)

    codes = [dest[b] for b in range(BLOCKS)]
    wide = lax.broadcasted_iota(jnp.int32, (8, 128), 1)
    owner = wide >> 3
    code = jnp.zeros((8, 128), jnp.int32)
    for b in range(BLOCKS):
        code = jnp.where(owner == b, codes[b], code)
    rank = jnp.zeros((8, 128), jnp.int32)
    for b in range(BLOCKS):
        rank = rank + jnp.where((code == codes[b]) & (owner > b), 1, 0)
    lanes_of = jnp.where(code < 13, code, code - 1) * 2 + rank
    key = jnp.where(code == 13, -1, lanes_of * 8 + (wide & 7))[0:1, :]
    value = states[...]
    part_0 = value.astype(bf16)
    value = value - part_0.astype(f32)
    part_1 = value.astype(bf16)
    part_2 = (value - part_1.astype(f32)).astype(bf16)
    chosen = jnp.where(lax.broadcasted_iota(jnp.int32, (416, 128), 0) == key, 1.0, 0.0).astype(bf16)
    outbox[...] = (
        jnp.dot(chosen, part_0, preferred_element_type=f32)
        + jnp.dot(chosen, part_1, preferred_element_type=f32)
        + jnp.dot(chosen, part_2, preferred_element_type=f32)
    )
    def over_droplets(source, weight):
        return lax.dot_general(source, weight, (((1,), (1,)), ((), ())), preferred_element_type=f32)

    last = over_droplets(slo[...], jnp.concatenate([weights[pl.ds(0, 128), :], weights[pl.ds(256, 128), :]], axis=0))
    part_high = over_droplets(shi[...], weights[pl.ds(256, 128), :])
    f_beyond[...] = part_high + last[:, 128:256]
    near = over_droplets(shi[pl.ds(192, 192), :], weights[pl.ds(0, 256), :])
    f_main[pl.ds(192, 192), :] = near[:, 0:128] + near[:, 128:256] + last[192:384, 0:128]
    f_main[pl.ds(0, 192), :] = last[0:192, 0:128]
    shifted = lane - 80
    spot = jnp.where(lane < 36, third, jnp.where((lane >= 80) & (lane < 116), (shifted * 171) >> 9, -1))

    f_copies = []
    for n, region in enumerate(region_list):
        first, count = regions[region]
        packed = None
        for g in range(0, count, GROUP):
            value = jnp.zeros((8, 128), f32)
            for k in range(g, min(g + GROUP, count)):
                rows = tile_rows(first + k)
                if region != (0, 0):
                    fsend[tile_rows(first - 24 + k), :] = f_main[rows, :]
                both = f_beyond[rows, :]
                value = jnp.where(spot == k - g, pltpu.roll(both, 3 * (k - g), 1) if k > g else both, value)
            value = value + pltpu.roll(value, 48, 1)
            packed = value if g == 0 else jnp.where(lane < 3 * g, packed, pltpu.roll(value, 3 * g, 1))
        fpsend[tile_rows(n), :] = packed
        back = (-region[0], -region[1])
        for side, dx in ((0, -1), (1, 1)):
            part = pl.ds(n * 8, 8)
            f_copies.append(copy(number, fpsend.at[part], fprecv.at[side, part], (-dx,) + back))
            number += 1
        if region != (0, 0):
            part = pl.ds((first - 24) * 8, count * 8)
            f_copies.append(copy(number, fsend.at[part], frecv.at[part], (0,) + back))
            number += 1

    h_copies = []
    for d in far_first:
        part = pl.ds(all_dirs.index(d) * 16, 16)
        h_copies.append(copy(number, outbox.at[part], inbox.at[part], d))
        number += 1

    near = over_droplets(shi[pl.ds(0, 192), :], weights[pl.ds(0, 256), :])
    f_main[pl.ds(0, 192), :] += near[:, 0:128] + near[:, 128:256]

    stay_rows = lax.broadcasted_iota(jnp.int32, (16, 128), 0)
    stays = jnp.zeros((16, 128), jnp.int32)
    for b in range(BLOCKS):
        stays = jnp.where(stay_rows == b, codes[b], stays)
    for c in range(6):
        arrived[c, pl.ds(0, 16), :] = jnp.where(stays == 13, states[pl.ds(c, 16, stride=8), :], 0.0)

    for made in started[waited : waited + 26]:
        made.wait_send()
    for made in f_copies:
        made.wait_recv()
    for n, region in enumerate(region_list):
        first, count = regions[region]
        merged = jnp.where(outer_low, fprecv[1, tile_rows(n), :], fprecv[0, tile_rows(n), :])
        for k in range(count):
            value = jnp.where((lane < 2) | (lane == 127), pltpu.roll(merged, (127 - 3 * k) % 128, 1), 0.0)
            rows = tile_rows(first + k)
            if region == (0, 0):
                f_main[rows, :] += value
            else:
                vmain[rows, :] = frecv[tile_rows(first - 24 + k), :] + value

    def row_of(t, r):
        return vmain[pl.ds(t * 8 + r, 1), :]

    def corner_row(region, c, y, z):
        return row_of(regions[region][0], corner_rows(region).index((c, y, z)))

    for c in range(3):
        for z in range(8):
            total = f_main[tile_rows(c * 8 + z), :]
            lines = [row_of(24 + c * 2, z), row_of(25 + c * 2, z), row_of(30 + c, z)]
            if z < 2 or z == 7:
                if z < 2:
                    total = total + vmain[tile_rows(33 + c * 2 + z), :]
                    low, high = (-1, -1), (1, -1)
                else:
                    total = total + vmain[tile_rows(39 + c), :]
                    low, high = (-1, 1), (1, 1)
                lines[0] = lines[0] + corner_row(low, c, 0, z)
                lines[1] = lines[1] + corner_row(low, c, 1, z)
                lines[2] = lines[2] + corner_row(high, c, 7, z)
            beside = jnp.where(sub == 0, lines[0], jnp.where(sub == 1, lines[1], jnp.where(sub == 7, lines[2], 0.0)))
            force[c, tile_rows(z), :] = total + beside

    for made in h_copies:
        made.wait_recv()
    for c in range(6):
        arrived[c, pl.ds(16, 52), :] = inbox[pl.ds(c, 52, stride=8), :]
    for made in started[waited + 26 :]:
        made.wait_send()


def deliver(state, force, arrived, state_hbm, force_hbm, arrived_hbm, sem):
    pairs = [(state.at[pl.ds(i, min(4, 19 - i))], state_hbm.at[pl.ds(i, min(4, 19 - i))]) for i in range(0, 19, 4)]
    pairs += [(arrived, arrived_hbm), (force, force_hbm)]
    copies = [pltpu.make_async_copy(src, dst, sem.at[n]) for n, (src, dst) in enumerate(pairs)]
    for made in copies:
        made.start()
    for made in copies:
        made.wait()


def solution(mesh):
    sizes = tuple(mesh.shape[a] for a in ("gx", "gy", "gz"))

    def body(*refs):
        kernel(sizes, *refs)

    def local(pops, coarse_pops, interface, drop_vel, drop_frac, home, counts, dest):
        vmem = pl.BlockSpec(memory_space=pltpu.VMEM)
        anywhere = pl.BlockSpec(memory_space=pl.ANY)
        made = pl.pallas_call(
            body,
            out_shape=(
                pltpu.VMEM((19, 64, 128), f32),
                pltpu.VMEM((3, 64, 128), f32),
                pltpu.VMEM((6, 68, 128), f32),
            ),
            in_specs=[pl.BlockSpec(memory_space=pltpu.HBM)] * 8,
            out_specs=(vmem, vmem, vmem),
            scratch_shapes=[
                pltpu.VMEM((19, 64, 128), f32),
                pltpu.VMEM((19, 8, 8, 128), bf16),
                pltpu.VMEM((8, 8, 128), jnp.int32),
                pltpu.VMEM((3, 16, 128), f32),
                pltpu.VMEM((3, 16, 128), f32),
                pltpu.VMEM((16, 128), jnp.int32),
                pltpu.SMEM((BLOCKS,), jnp.int32),
                pltpu.SMEM((BLOCKS,), jnp.int32),
                pltpu.VMEM((19, 64, 128), f32),
                pltpu.VMEM((19, 64, 128), f32),
                pltpu.VMEM((2, POST_TILES * 8, 128), f32),
                pltpu.VMEM((2, POST_TILES * 8, 128), f32),
                pltpu.VMEM((ROWS, 128), f32),
                pltpu.VMEM((24 * 8, 128), f32),
                pltpu.VMEM((72, 128), f32),
                pltpu.VMEM((2, 72, 128), f32),
                pltpu.VMEM((ROWS, 256), bf16),
                pltpu.VMEM((ROWS, 256), bf16),
                pltpu.VMEM((384, WIDE), bf16),
                pltpu.VMEM((12, 16, 128), f32),
                pltpu.VMEM((3, 16, 128), jnp.int32),
                pltpu.VMEM((BLOCKS, U_TILES * 8, 128), f32),
                pltpu.VMEM((PAIRS, 192, 256), f32),
                pltpu.VMEM((BLOCKS, 24, 128), f32),
                pltpu.VMEM((ROWS, WIDE), bf16),
                pltpu.VMEM((ROWS, WIDE), bf16),
                pltpu.VMEM((ROWS, 128), f32),
                pltpu.VMEM((ROWS, 128), f32),
                pltpu.VMEM((24 * 8, 128), f32),
                pltpu.VMEM((24 * 8, 128), f32),
                pltpu.VMEM((72, 128), f32),
                pltpu.VMEM((2, 72, 128), f32),
                pltpu.VMEM((BLOCKS * 8, 128), f32),
                pltpu.VMEM((416, 128), f32),
                pltpu.VMEM((416, 128), f32),
                pltpu.SemaphoreType.DMA((N_MSG,)),
                pltpu.SemaphoreType.DMA((N_MSG,)),
                pltpu.SemaphoreType.DMA((8,)),
            ],
            compiler_params=pltpu.CompilerParams(
                collective_id=0, has_side_effects=True, vmem_limit_bytes=36 * 1024 * 1024
            ),
            name="channel",
        )(
            *(
                pltpu.with_memory_space_constraint(x, pltpu.HBM)
                for x in (pops.reshape(19, 64, 128), coarse_pops, interface, drop_vel, drop_frac, home, counts, dest)
            )
        )
        state, force, arrived = pl.pallas_call(
            deliver,
            out_shape=(
                jax.ShapeDtypeStruct((19, 64, 128), f32),
                jax.ShapeDtypeStruct((3, 64, 128), f32),
                jax.ShapeDtypeStruct((6, 68, 128), f32),
            ),
            in_specs=[vmem] * 3,
            out_specs=(anywhere,) * 3,
            scratch_shapes=[pltpu.SemaphoreType.DMA((7,))],
            compiler_params=pltpu.CompilerParams(vmem_limit_bytes=8 * 1024 * 1024),
            name="deliver",
        )(*made)
        return state.reshape(19, 8, 8, 128), force.reshape(3, 8, 8, 128), arrived

    return jax.shard_map(
        local,
        mesh=mesh,
        in_specs=(
            P(None, "gz", "gy", "gx"),
            P(None, "gz", "gy", "gx"),
            P("gz", "gy", "gx"),
            P(None, ("gx", "gy", "gz"), None),
            P(None, ("gx", "gy", "gz"), None),
            P(("gx", "gy", "gz"), None),
            P(("gx", "gy", "gz")),
            P(("gx", "gy", "gz")),
        ),
        out_specs=(
            P(None, "gz", "gy", "gx"),
            P(None, "gz", "gy", "gx"),
            P(None, ("gx", "gy", "gz"), None),
        ),
        check_vma=False,
    )
```

```python
import math

import jax
import jax.numpy as jnp
import numpy as np
from jax import lax
from jax.experimental import pallas as pl
from jax.experimental.pallas import tpu as pltpu
from jax.sharding import PartitionSpec as P

lattice = [
    (0, 0, 0), (1, 0, 0), (-1, 0, 0), (0, 1, 0), (0, -1, 0), (0, 0, 1), (0, 0, -1),
    (1, 1, 0), (-1, -1, 0), (1, -1, 0), (-1, 1, 0), (1, 0, 1), (-1, 0, -1), (1, 0, -1),
    (-1, 0, 1), (0, 1, 1), (0, -1, -1), (0, 1, -1), (0, -1, 1),
]
weights_table = [1.0 / 3.0] + [1.0 / 18.0] * 6 + [1.0 / 36.0] * 12
opposite = [0, 2, 1, 4, 3, 6, 5, 8, 7, 10, 9, 12, 11, 14, 13, 16, 15, 18, 17]
inverse_tau = 0.8
relax = 0.5
couple = 8.0
f32 = jnp.float32
bf16 = jnp.bfloat16

face_pops = {}
for axis in range(3):
    for sign in (1, -1):
        d = [0, 0, 0]
        d[axis] = sign
        face_pops[tuple(d)] = [i for i in range(19) if lattice[i][axis] == sign]
post_msgs = {}
tiles = 0
for i in list(range(7, 19)) + [3, 4, 5, 6, 1, 2]:
    c = lattice[i]
    count = 1 if (abs(c[0]) + abs(c[1]) + abs(c[2]) > 1 or c[0] != 0) else 5
    post_msgs[c] = (tiles, count)
    tiles += count
POST_TILES = tiles

regions = {
    (0, 0): (0, 24),
    (-1, 0): (24, 6),
    (1, 0): (30, 3),
    (0, -1): (33, 6),
    (0, 1): (39, 3),
    (-1, -1): (42, 2),
    (1, -1): (44, 1),
    (-1, 1): (45, 1),
    (1, 1): (46, 1),
}
region_list = list(regions)[::-1]
ROWS = 48 * 8
all_dirs = [(x, y, z) for z in (-1, 0, 1) for y in (-1, 0, 1) for x in (-1, 0, 1) if (x, y, z) != (0, 0, 0)]
far_first = sorted(all_dirs, key=lambda d: -abs(d[0]) - abs(d[1]) - abs(d[2]))
near_dirs = [d for d in far_first if 0 in d]
U_TILES = 19
WIDE = 2048
N_POST = 18
N_MSG = 2 * N_POST + 3 * 26
PAIRS = 8
BLOCKS = 16
UNROLL = 4
GROUP = 12


def corner_rows(region):
    dy, dz = region
    ys = [7] if dy == 1 else [0, 1]
    zs = [7] if dz == 1 else [0, 1]
    return [(c, y, z) for c in range(3) for z in zs for y in ys]


def tile_rows(t):
    return pl.ds(t * 8, 8)


def kernel(
    sizes,
    pops_hbm, coarse_hbm, interface_hbm, drop_vel_hbm, drop_frac_hbm, home_hbm, counts_hbm, dest_hbm,
    state_out, force, arrived,
    pops, coarse, interface, drop_vel, drop_frac, home, counts, dest,
    posts, state_mid, psend, precv, vmain, vsend, pksend, pkrecv, va, vb, weights,
    taps, homes, spread_weights, tmain, partial, shi, slo, f_main, f_beyond, fsend, frecv, fpsend, fprecv, states, outbox, inbox,
    send_sem, recv_sem, in_sem,
):
    n_x, n_y, n_z = sizes
    me = (lax.axis_index("gx"), lax.axis_index("gy"), lax.axis_index("gz"))
    level = me[2]
    at_bottom = level == 0
    at_top = level == n_z - 1

    def moved_by(axis, step, size):
        if step == 0:
            return me[axis]
        return lax.rem(me[axis] + (step + size), size)

    coords = {
        (axis, step): moved_by(axis, step, size)
        for axis, size in enumerate(sizes)
        for step in (-1, 0, 1)
    }

    def device(d):
        return {"gx": coords[0, d[0]], "gy": coords[1, d[1]], "gz": coords[2, d[2]]}

    lane = lax.broadcasted_iota(jnp.int32, (8, 128), 1)
    sub = lax.broadcasted_iota(jnp.int32, (8, 128), 0)

    third = (lane * 171) >> 9
    outer_low = lane - third * 3 == 0
    started = []

    def copy(index, src, dst, d):
        made = pltpu.make_async_remote_copy(
            src_ref=src,
            dst_ref=dst,
            send_sem=send_sem.at[index],
            recv_sem=recv_sem.at[index],
            device_id=device(d),
            device_id_type=pl.DeviceIdType.MESH,
        )
        made.start()
        started.append(made)
        return made

    barrier = pltpu.get_barrier_semaphore()
    for d in near_dirs:
        pl.semaphore_signal(barrier, inc=1, device_id=device(d), device_id_type=pl.DeviceIdType.MESH)

    loads = []
    for n, (src, dst) in enumerate(
        (
            (pops_hbm, pops),
            (coarse_hbm, coarse),
            (interface_hbm, interface),
            (drop_vel_hbm, drop_vel),
            (drop_frac_hbm, drop_frac),
            (home_hbm, home),
            (counts_hbm, counts),
            (dest_hbm, dest),
        )
    ):
        loads.append(pltpu.make_async_copy(src, dst, in_sem.at[n]))
        loads[-1].start()
    def macroscopic(values):
        plus = {i: values[i] + values[i + 1] for i in range(1, 19, 2)}
        minus = {i: values[i] - values[i + 1] for i in range(1, 19, 2)}
        axes = plus[1] + plus[3] + plus[5]
        edges = (plus[7] + plus[9]) + (plus[11] + plus[13]) + (plus[15] + plus[17])
        density = values[0] * weights_table[0] + axes * weights_table[1] + edges * weights_table[7]
        inverse = 1.0 / density
        near, far = weights_table[1] * inverse, weights_table[7] * inverse
        flow = [
            minus[1] * near + ((minus[7] + minus[9]) + (minus[11] + minus[13])) * far,
            minus[3] * near + ((minus[7] - minus[9]) + (minus[15] + minus[17])) * far,
            minus[5] * near + ((minus[11] - minus[13]) + (minus[15] - minus[17])) * far,
        ]
        return density, flow

    def collide(source):
        @pl.loop(0, 8, unroll=2)
        def _(z):
            rows = pl.ds(pl.multiple_of(z * 8, 8), 8)
            values = [source[i, rows, :] for i in range(19)]
            density, flow = macroscopic(values)
            square = flow[0] * flow[0] + flow[1] * flow[1] + flow[2] * flow[2]
            inside = interface[z] == 1
            scaled = density * inverse_tau
            base = scaled - square * (1.5 * scaled)
            first, second = scaled * 3.0, scaled * 4.5

            def put(i, balance):
                relaxed = values[i] * (1.0 - inverse_tau) + balance
                posts[i, rows, :] = jnp.where(inside, coarse[i, z].astype(f32), relaxed)

            put(0, base)
            for i in range(1, 19, 2):
                along = None
                for axis in range(3):
                    sign = lattice[i][axis]
                    if sign == 1:
                        along = flow[axis] if along is None else along + flow[axis]
                    if sign == -1:
                        along = along - flow[axis]
                even = base + along * along * second
                odd = along * first
                put(i, even + odd)
                put(i + 1, even - odd)

    def pack_posts(r, part):
        for d, (first, count) in list(post_msgs.items())[part]:
            layer = {a: (7 if d[a] == 1 else 0) for a in (1, 2)}
            if d in face_pops:
                listed = face_pops[d]
            else:
                listed = [lattice.index(d)]
            if d[0] != 0 and d[1] == 0 and d[2] == 0:
                acc = jnp.zeros((8, 128), f32)
                from_lane = 127 if d[0] == 1 else 0
                for k, i in enumerate(listed):
                    for z in range(8):
                        spot = k * 8 + z
                        turned = pltpu.roll(posts[i, tile_rows(z), :], (spot - from_lane) % 128, 1)
                        acc = jnp.where(lane == spot, turned, acc)
                psend[r, tile_rows(first), :] = acc
            elif d[2] != 0:
                for k, i in enumerate(listed):
                    psend[r, tile_rows(first + k), :] = posts[i, tile_rows(layer[2]), :]
            else:
                for k, i in enumerate(listed):
                    psend[r, tile_rows(first + k), :] = posts[i, pl.ds(layer[1], 8, stride=8), :]

    edges, faces = slice(0, 12), slice(12, 18)

    def send_posts(r, part):
        for d, (first, count) in list(post_msgs.items())[part]:
            rows = pl.ds(first * 8, count * 8)
            post_copies[r].append(copy(len(started), psend.at[r, rows], precv.at[r, rows], d))

    post_copies = ([], [])

    def pull(r, i):
        cx, cy, cz = lattice[i]
        far = 127 if cx == 1 else 0

        def halo(d):
            first, count = post_msgs[d]
            k = face_pops[d].index(i) if d in face_pops and d[0] == 0 else 0
            return first + k

        def x_shift(value, beyond):
            return pltpu.roll(jnp.where(lane == far, beyond, value), cx % 128, 1)

        def y_shift(value, row):
            edge = 0 if cy == 1 else 7
            return jnp.where(sub == edge, row, pltpu.roll(value, cy % 8, 0))

        wanted = [z - cz for z in range(8)]
        planes = {z: posts[i, tile_rows(z), :] for z in range(8) if z in wanted}
        outer = None
        if cz != 0:
            outer = precv[r, tile_rows(halo((0, 0, cz))), :]
        if cx != 0:
            packed = precv[r, tile_rows(post_msgs[(cx, 0, 0)][0]), :]
            k = face_pops[(cx, 0, 0)].index(i)
            for z in planes:
                planes[z] = x_shift(planes[z], pltpu.roll(packed, (far - (k * 8 + z)) % 128, 1))
            if cz != 0:
                outer = x_shift(outer, precv[r, tile_rows(halo((cx, 0, cz))), :])
        if cy != 0:
            place = halo((0, cy, 0))
            if cx != 0:
                side = x_shift(precv[r, tile_rows(place), :], precv[r, tile_rows(halo((cx, cy, 0))), :])
                for z in planes:
                    planes[z] = y_shift(planes[z], side[z : z + 1, :])
            else:
                for z in planes:
                    planes[z] = y_shift(planes[z], precv[r, pl.ds(place * 8 + z, 1), :])
            if cz != 0:
                row = halo((0, cy, cz)) * 8 + (7 if cy == 1 else 0)
                outer = y_shift(outer, precv[r, pl.ds(row, 1), :])
        out = [planes[z] if z in planes else outer for z in wanted]
        if cz == 1:
            out[0] = jnp.where(at_bottom, posts[opposite[i], tile_rows(0), :], out[0])
        if cz == -1:
            out[7] = jnp.where(at_top, posts[opposite[i], tile_rows(7), :], out[7])
        return out

    def stream(r, copies, into):
        for made in copies:
            made.wait_recv()
        for i in range(19):
            out = pull(r, i)
            for z in range(8):
                into[i, tile_rows(z), :] = out[z]

    def prepare():
        for axis in range(3):
            angle = drop_frac[axis] * (0.5 * math.pi)
            sine = jnp.sin(angle)
            cosine = jnp.cos(angle)
            taps[axis * 4 + 0] = 0.25 - 0.25 * sine
            taps[axis * 4 + 1] = 0.25 + 0.25 * cosine
            taps[axis * 4 + 2] = 0.25 + 0.25 * sine
            taps[axis * 4 + 3] = 0.25 - 0.25 * cosine
        cells = home[...]
        homes[0] = (cells & 127) - 1
        homes[1] = ((cells >> 7) & 7) - 1
        homes[2] = (cells >> 10) - 1

    def picked(offset, weight):
        zero = jnp.zeros(offset.shape, f32)
        return jnp.where(
            offset == 0,
            weight[0],
            jnp.where(offset == 1, weight[1], jnp.where(offset == 2, weight[2], jnp.where(offset == 3, weight[3], zero))),
        )

    rows16 = lax.broadcasted_iota(jnp.int32, (16, 128), 0)

    def build_x_weights():
        @pl.loop(0, BLOCKS)
        def _(b):
            block = pl.ds(b, 1)
            lanes = pl.ds(pl.multiple_of(b * 128, 128), 128)
            first = homes[0, block, :]
            weight = [taps[k, block, :] for k in range(4)]
            for t in range(8):
                value = picked(rows16 + t * 16 - first, weight)
                high_part = value.astype(bf16)
                weights[pl.ds(t * 16, 16), lanes] = high_part
                weights[pl.ds(128 + t * 16, 16), lanes] = (value - high_part.astype(f32)).astype(bf16)
            def outside(at):
                row = rows16 - at
                cell = jnp.where(row == 0, -1, jnp.where(row == 1, 128, jnp.where(row == 2, 129, -1000)))
                return picked(cell - first, weight)

            value = outside(0)
            high_part = value.astype(bf16)
            weights[pl.ds(256, 16), lanes] = high_part
            weights[pl.ds(272, 16), lanes] = jnp.zeros((16, 128), bf16)
            weights[pl.ds(288, 16), lanes] = outside(8).astype(bf16)
            weights[pl.ds(304, 32), lanes] = jnp.zeros((32, 128), bf16)
            weights[pl.ds(336, 16), lanes] = (value - high_part.astype(f32)).astype(bf16)
            weights[pl.ds(352, 32), lanes] = jnp.zeros((32, 128), bf16)

    def build_yz_weights():
        @pl.loop(0, BLOCKS)
        def _(b):
            block = pl.ds(b, 1)
            hy = homes[1, block, :]
            hz = homes[2, block, :]
            wy = [taps[4 + k, block, :] for k in range(4)]
            wz = [taps[8 + k, block, :] for k in range(4)]
            y_main = picked(sub - hy, wy)
            z_main = picked(sub - hz, wz)
            y_out = [picked(y - hy, wy) for y in (8, 9, -1)]
            z_out = [picked(z - hz, wz) for z in (8, 9, -1)]
            z_out = [jnp.where(at_top, 0.0, z_out[0]), jnp.where(at_top, 0.0, z_out[1]), jnp.where(at_bottom, 0.0, z_out[2])]
            even = (sub & 1) == 0
            y_pair = jnp.where(even, y_out[0], y_out[1])
            z_pair = jnp.where(even, z_out[0], z_out[1])
            both = y_pair * jnp.where((sub & 2) == 0, z_out[0], z_out[1])
            made = [y_main * z_main[z : z + 1, :] for z in range(8)]
            made += [z_main * y_out[k] for k in range(3)]
            made += [y_main * z_out[k] for k in range(3)]
            made.append(both)
            made.append(jnp.where(sub < 4, both, 0.0))
            made.append(jnp.where(sub < 6, y_out[2] * z_pair, 0.0))
            made.append(jnp.where(sub < 6, y_pair * z_out[2], 0.0))
            made.append(jnp.where(sub < 3, y_out[2] * z_out[2], 0.0))
            for t in range(U_TILES):
                spread_weights[b, tile_rows(t), :] = made[t]

    for made in loads[:3]:
        made.wait()
    collide(pops)
    pack_posts(0, edges)
    pack_posts(0, faces)
    pl.semaphore_wait(barrier, len(near_dirs))
    send_posts(0, edges)
    send_posts(0, faces)
    stream(0, post_copies[0], state_mid)
    collide(state_mid)
    pack_posts(1, edges)
    send_posts(1, edges)
    pack_posts(1, faces)
    send_posts(1, faces)
    for made in loads[3:]:
        made.wait()
    prepare()
    build_x_weights()
    build_yz_weights()
    stream(1, post_copies[1], state_out)

    for z in range(8):
        values = [state_out[i, tile_rows(z), :] for i in range(19)]
        flow = macroscopic(values)[1]
        for c in range(3):
            vmain[tile_rows(c * 8 + z), :] = flow[c]

    def sent_tile(region, k):
        dy, dz = region
        if region == (0, 0):
            return vmain[tile_rows(k), :]
        if dz == 0:
            start = (k // 2) * 64 + k % 2 if dy == -1 else k * 64 + 7
            return vmain[pl.ds(start, 8, stride=8), :]
        if dy == 0:
            tile = (k // 2) * 8 + k % 2 if dz == -1 else k * 8 + 7
            return vmain[tile_rows(tile), :]
        acc = jnp.zeros((8, 128), f32)
        for r, (c, y, z) in enumerate(corner_rows(region)[k * 8 : k * 8 + 8]):
            acc = jnp.where(sub == r, vmain[pl.ds(c * 64 + z * 8 + y, 1), :], acc)
        return acc

    v_copies = {1: [], 2: [], 3: []}
    for n, region in enumerate(region_list):
        first, count = regions[region]
        packed = jnp.zeros((8, 128), f32)
        for k in range(count):
            value = sent_tile(region, k)
            if region != (0, 0):
                vsend[tile_rows(first - 24 + k), :] = value
            packed = jnp.where(third == k, pltpu.roll(value, 3 * k + 1, 1), packed)
        pksend[tile_rows(n), :] = packed
        for side, dx in ((0, -1), (1, 1)):
            part = pl.ds(n * 8, 8)
            made = copy(len(started), pksend.at[part], pkrecv.at[side, part], (dx,) + region)
            v_copies[1 + abs(region[0]) + abs(region[1])].append(made)
        if region != (0, 0):
            part = pl.ds((first - 24) * 8, count * 8)
            made = copy(len(started), vsend.at[part], vmain.at[pl.ds(first * 8, count * 8)], (0,) + region)
            v_copies[abs(region[0]) + abs(region[1])].append(made)

    def split_main(low, high):
        for t in range(low, high):
            rows = pl.ds(t * 16, 16)
            value = vmain[rows, :]
            high_part = value.astype(bf16)
            va[rows, pl.ds(0, 128)] = high_part
            vb[rows, pl.ds(0, 128)] = high_part
            va[rows, pl.ds(128, 128)] = (value - high_part.astype(f32)).astype(bf16)

    vmain[tile_rows(47), :] = jnp.zeros((8, 128), f32)
    split_main(0, 12)

    @pl.loop(0, PAIRS)
    def _(p):
        lanes = pl.ds(pl.multiple_of(p * 256, 256), 256)
        w_high = weights[pl.ds(0, 128), lanes]
        tmain[p] = jnp.dot(va[pl.ds(0, 192), :], jnp.concatenate([w_high, w_high], axis=0), preferred_element_type=f32)

    waited = 2 * N_POST
    for made in started[:waited]:
        made.wait_send()
    def unpack(n, region):
        first, count = regions[region]
        merged = jnp.where(outer_low, pkrecv[1, tile_rows(n), :], pkrecv[0, tile_rows(n), :])
        for g in range(0, count, GROUP):
            value = merged if g == 0 else pltpu.roll(merged, (-3 * g) % 128, 1)
            high_part = value.astype(bf16).astype(f32)
            low_part = pltpu.roll(value - high_part, 40, 1)
            value = jnp.where(lane < 40, high_part, jnp.where(lane < 80, low_part, pltpu.roll(high_part, 80, 1)))
            for k in range(g, min(g + GROUP, count)):
                beyond[first + k] = pltpu.roll(value, (-3 * (k - g)) % 128, 1) if k > g else value

    def store_beyond(low, high):
        for t in range(low, high):
            vb[pl.ds(t * 16, 16), pl.ds(128, 128)] = jnp.concatenate([beyond[2 * t], beyond[2 * t + 1]], axis=0).astype(bf16)

    beyond = {47: jnp.zeros((8, 128), f32)}
    for made in v_copies[1]:
        made.wait_recv()
    split_main(12, 21)
    unpack(region_list.index((0, 0)), (0, 0))
    store_beyond(0, 12)

    @pl.loop(0, PAIRS, unroll=UNROLL)
    def _(p):
        pair_lanes = pl.ds(pl.multiple_of(p * 256, 256), 256)
        w_high = weights[pl.ds(0, 128), pair_lanes]
        t_main = tmain[p] + jnp.dot(
            vb[pl.ds(0, 192), :], weights[pl.ds(128, 256), pair_lanes], preferred_element_type=f32
        )
        t_face = jnp.dot(
            va[pl.ds(192, 144), :], jnp.concatenate([w_high, w_high], axis=0), preferred_element_type=f32
        ) + jnp.dot(
            vb[pl.ds(192, 144), pl.ds(0, 128)], weights[pl.ds(128, 128), pair_lanes], preferred_element_type=f32
        )
        for j in range(2):
            b = 2 * p + j

            def tile(t):
                source, at = (t_main, t) if t < 24 else (t_face, t - 24)
                return source[at * 8 : at * 8 + 8, j * 128 : (j + 1) * 128]

            def u(t):
                return spread_weights[b, tile_rows(t), :]

            for c in range(3):
                acc = tile(24 + c * 2) * u(8) + tile(25 + c * 2) * u(9) + tile(30 + c) * u(10)
                acc = acc + tile(33 + c * 2) * u(11) + tile(34 + c * 2) * u(12) + tile(39 + c) * u(13)
                other = tile(c * 8) * u(0)
                for z in range(1, 8):
                    other = other + tile(c * 8 + z) * u(z)
                partial[b, tile_rows(c), :] = acc + other

    def corner_terms(tile, u):
        p42 = tile(42) * u(14)
        p43 = tile(43) * u(15)
        p445 = tile(44) * u(16) + tile(45) * u(17)
        p46 = tile(46) * u(18)
        terms = []
        for c in range(3):
            acc = jnp.where((sub >> 1) == c, p445, 0.0) + jnp.where(sub == c, p46, 0.0)
            terms.append(acc + (jnp.where((sub >> 2) == c, p42, 0.0) if c < 2 else p43))
        return terms

    for made in v_copies[2]:
        made.wait_recv()
    split_main(21, 24)
    for n, region in enumerate(region_list):
        if abs(region[0]) + abs(region[1]) == 1:
            unpack(n, region)
    store_beyond(12, 21)

    @pl.loop(0, PAIRS, unroll=UNROLL)
    def _(p):
        pair_lanes = pl.ds(pl.multiple_of(p * 256, 256), 256)
        w_high = weights[pl.ds(0, 128), pair_lanes]
        t_side = jnp.dot(
            vb[pl.ds(192, 144), pl.ds(128, 128)], weights[pl.ds(256, 128), pair_lanes], preferred_element_type=f32
        )
        t_corner = jnp.dot(
            va[pl.ds(336, 48), :], jnp.concatenate([w_high, w_high], axis=0), preferred_element_type=f32
        ) + jnp.dot(
            vb[pl.ds(336, 48), pl.ds(0, 128)], weights[pl.ds(128, 128), pair_lanes], preferred_element_type=f32
        )
        for j in range(2):
            b = 2 * p + j

            def tile(t):
                source, at = (t_side, t - 24) if t < 42 else (t_corner, t - 42)
                return source[at * 8 : at * 8 + 8, j * 128 : (j + 1) * 128]

            def u(t):
                return spread_weights[b, tile_rows(t), :]

            for c, acc in enumerate(corner_terms(tile, u)):
                acc = acc + tile(24 + c * 2) * u(8) + tile(25 + c * 2) * u(9) + tile(30 + c) * u(10)
                acc = acc + tile(33 + c * 2) * u(11) + tile(34 + c * 2) * u(12) + tile(39 + c) * u(13)
                partial[b, tile_rows(c), :] += acc

    for made in v_copies[3]:
        made.wait_recv()
    for n, region in enumerate(region_list):
        if abs(region[0]) + abs(region[1]) == 2:
            unpack(n, region)
    store_beyond(21, 24)

    @pl.loop(0, PAIRS, unroll=UNROLL)
    def _(p):
        pair_lanes = pl.ds(pl.multiple_of(p * 256, 256), 256)
        t_corner = jnp.dot(
            vb[pl.ds(336, 48), pl.ds(128, 128)], weights[pl.ds(256, 128), pair_lanes], preferred_element_type=f32
        )
        for j in range(2):
            b = 2 * p + j
            lanes = pl.ds(pl.multiple_of(p * 256 + j * 128, 128), 128)
            block = pl.ds(b, 1)

            def tile(t):
                return t_corner[(t - 42) * 8 : (t - 41) * 8, j * 128 : (j + 1) * 128]

            def u(t):
                return spread_weights[b, tile_rows(t), :]

            terms = corner_terms(tile, u)
            alive = lax.broadcasted_iota(jnp.int32, (1, 128), 1) < counts[b]
            pushes = []
            rows = []
            for c in range(3):
                acc = terms[c] + partial[b, tile_rows(c), :]
                sampled = jnp.sum(acc, axis=0, keepdims=True)
                speed = drop_vel[c, block, :]
                moved = speed + relax * (sampled - speed)
                pushes.append(jnp.where(alive, couple * (moved - sampled), 0.0))
                rows.append(jnp.where(alive, moved, 0.0))
            for c in range(3):
                rows.append(jnp.where(alive, drop_frac[c, block, :], 0.0) + rows[c])
            block_state = jnp.zeros((8, 128), f32)
            for c in range(6):
                block_state = jnp.where(sub == c, rows[c], block_state)
            states[pl.ds(pl.multiple_of(b * 8, 8), 8), :] = block_state

            by_half = jnp.where((sub >> 1) == 0, pushes[0], jnp.where((sub >> 1) == 1, pushes[1], pushes[2]))
            by_row = jnp.where(sub == 0, pushes[0], jnp.where(sub == 1, pushes[1], pushes[2]))
            by_four = jnp.where(sub < 4, pushes[0], pushes[1])
            plan = [(pushes[c], z) for c in range(3) for z in range(8)]
            plan += [(pushes[c], 8 + k) for c in range(3) for k in range(2)]
            plan += [(pushes[c], 10) for c in range(3)]
            plan += [(pushes[c], 11 + k) for c in range(3) for k in range(2)]
            plan += [(pushes[c], 13) for c in range(3)]
            plan += [(by_four, 14), (pushes[2], 15), (by_half, 16), (by_half, 17), (by_row, 18)]
            sources = [push * u(t) for push, t in plan] + [jnp.zeros((8, 128), f32)]
            for t in range(ROWS // 16):
                value = jnp.concatenate([sources[2 * t], sources[2 * t + 1]], axis=0)
                high_part = value.astype(bf16)
                shi[pl.ds(t * 16, 16), lanes] = high_part
                slo[pl.ds(t * 16, 16), lanes] = (value - high_part.astype(f32)).astype(bf16)

    codes = [dest[b] for b in range(BLOCKS)]
    wide = lax.broadcasted_iota(jnp.int32, (8, 128), 1)
    owner = wide >> 3
    code = jnp.zeros((8, 128), jnp.int32)
    for b in range(BLOCKS):
        code = jnp.where(owner == b, codes[b], code)
    rank = jnp.zeros((8, 128), jnp.int32)
    for b in range(BLOCKS):
        rank = rank + jnp.where((code == codes[b]) & (owner > b), 1, 0)
    lanes_of = jnp.where(code < 13, code, code - 1) * 2 + rank
    key = jnp.where(code == 13, -1, lanes_of * 8 + (wide & 7))[0:1, :]
    value = states[...]
    part_0 = value.astype(bf16)
    value = value - part_0.astype(f32)
    part_1 = value.astype(bf16)
    part_2 = (value - part_1.astype(f32)).astype(bf16)
    chosen = jnp.where(lax.broadcasted_iota(jnp.int32, (416, 128), 0) == key, 1.0, 0.0).astype(bf16)
    outbox[...] = (
        jnp.dot(chosen, part_0, preferred_element_type=f32)
        + jnp.dot(chosen, part_1, preferred_element_type=f32)
        + jnp.dot(chosen, part_2, preferred_element_type=f32)
    )
    h_copies = []

    def hand_over(hops):
        for d in far_first:
            if abs(d[0]) + abs(d[1]) + abs(d[2]) == hops:
                part = pl.ds(all_dirs.index(d) * 16, 16)
                h_copies.append(copy(len(started), outbox.at[part], inbox.at[part], d))

    hand_over(3)

    def over_droplets(source, weight):
        return lax.dot_general(source, weight, (((1,), (1,)), ((), ())), preferred_element_type=f32)

    shifted = lane - 80
    spot = jnp.where(lane < 36, third, jnp.where((lane >= 80) & (lane < 116), (shifted * 171) >> 9, -1))

    f_copies = []
    thirds = weights[pl.ds(256, 128), :]

    def spread_rows(low, count):
        rows = pl.ds(low, count)
        near = over_droplets(shi[rows, :], weights[pl.ds(0, 256), :])
        last = over_droplets(slo[rows, :], jnp.concatenate([weights[pl.ds(0, 128), :], thirds], axis=0))
        f_beyond[rows, :] = over_droplets(shi[rows, :], thirds) + last[:, 128:256]
        f_main[rows, :] = near[:, 0:128] + near[:, 128:256] + last[:, 0:128]

    spread_rows(336, 48)
    done = 2
    for n, region in enumerate(region_list):
        first, count = regions[region]
        if abs(region[0]) + abs(region[1]) < done:
            hand_over(done)
            done -= 1
            if done == 1:
                spread_rows(192, 144)
            else:
                own = pl.ds(0, 192)
                f_beyond[own, :] = over_droplets(shi[own, :], thirds) + over_droplets(slo[own, :], thirds)
        packed = None
        for g in range(0, count, GROUP):
            value = jnp.zeros((8, 128), f32)
            for k in range(g, min(g + GROUP, count)):
                rows = tile_rows(first + k)
                if region != (0, 0):
                    fsend[tile_rows(first - 24 + k), :] = f_main[rows, :]
                both = f_beyond[rows, :]
                value = jnp.where(spot == k - g, pltpu.roll(both, 3 * (k - g), 1) if k > g else both, value)
            value = value + pltpu.roll(value, 48, 1)
            packed = value if g == 0 else jnp.where(lane < 3 * g, packed, pltpu.roll(value, 3 * g, 1))
        fpsend[tile_rows(n), :] = packed
        back = (-region[0], -region[1])
        for side, dx in ((0, -1), (1, 1)):
            part = pl.ds(n * 8, 8)
            f_copies.append(copy(len(started), fpsend.at[part], fprecv.at[side, part], (-dx,) + back))
        if region != (0, 0):
            part = pl.ds((first - 24) * 8, count * 8)
            f_copies.append(copy(len(started), fsend.at[part], frecv.at[part], (0,) + back))

    near = over_droplets(shi[own, :], weights[pl.ds(0, 256), :])
    last = over_droplets(slo[own, :], weights[pl.ds(0, 128), :])
    f_main[own, :] = near[:, 0:128] + near[:, 128:256] + last

    stay_rows = lax.broadcasted_iota(jnp.int32, (16, 128), 0)
    stays = jnp.zeros((16, 128), jnp.int32)
    for b in range(BLOCKS):
        stays = jnp.where(stay_rows == b, codes[b], stays)
    for c in range(6):
        arrived[c, pl.ds(0, 16), :] = jnp.where(stays == 13, states[pl.ds(c, 16, stride=8), :], 0.0)

    for made in started[waited : waited + 26]:
        made.wait_send()
    for made in f_copies:
        made.wait_recv()
    for n, region in enumerate(region_list):
        first, count = regions[region]
        merged = jnp.where(outer_low, fprecv[1, tile_rows(n), :], fprecv[0, tile_rows(n), :])
        for k in range(count):
            value = jnp.where((lane < 2) | (lane == 127), pltpu.roll(merged, (127 - 3 * k) % 128, 1), 0.0)
            rows = tile_rows(first + k)
            if region == (0, 0):
                f_main[rows, :] += value
            else:
                vmain[rows, :] = frecv[tile_rows(first - 24 + k), :] + value

    def row_of(t, r):
        return vmain[pl.ds(t * 8 + r, 1), :]

    def corner_row(region, c, y, z):
        return row_of(regions[region][0], corner_rows(region).index((c, y, z)))

    for c in range(3):
        for z in range(8):
            total = f_main[tile_rows(c * 8 + z), :]
            lines = [row_of(24 + c * 2, z), row_of(25 + c * 2, z), row_of(30 + c, z)]
            if z < 2 or z == 7:
                if z < 2:
                    total = total + vmain[tile_rows(33 + c * 2 + z), :]
                    low, high = (-1, -1), (1, -1)
                else:
                    total = total + vmain[tile_rows(39 + c), :]
                    low, high = (-1, 1), (1, 1)
                lines[0] = lines[0] + corner_row(low, c, 0, z)
                lines[1] = lines[1] + corner_row(low, c, 1, z)
                lines[2] = lines[2] + corner_row(high, c, 7, z)
            beside = jnp.where(sub == 0, lines[0], jnp.where(sub == 1, lines[1], jnp.where(sub == 7, lines[2], 0.0)))
            force[c, tile_rows(z), :] = total + beside

    for made in h_copies:
        made.wait_recv()
    for c in range(6):
        arrived[c, pl.ds(16, 52), :] = inbox[pl.ds(c, 52, stride=8), :]
    for made in started[waited + 26 :]:
        made.wait_send()


def deliver(state, force, arrived, state_hbm, force_hbm, arrived_hbm, sem):
    pairs = [(state.at[pl.ds(i, min(4, 19 - i))], state_hbm.at[pl.ds(i, min(4, 19 - i))]) for i in range(0, 19, 4)]
    pairs += [(arrived, arrived_hbm), (force, force_hbm)]
    copies = [pltpu.make_async_copy(src, dst, sem.at[n]) for n, (src, dst) in enumerate(pairs)]
    for made in copies:
        made.start()
    for made in copies:
        made.wait()


def solution(mesh):
    sizes = tuple(mesh.shape[a] for a in ("gx", "gy", "gz"))

    def body(*refs):
        kernel(sizes, *refs)

    def local(pops, coarse_pops, interface, drop_vel, drop_frac, home, counts, dest):
        vmem = pl.BlockSpec(memory_space=pltpu.VMEM)
        anywhere = pl.BlockSpec(memory_space=pl.ANY)
        made = pl.pallas_call(
            body,
            out_shape=(
                pltpu.VMEM((19, 64, 128), f32),
                pltpu.VMEM((3, 64, 128), f32),
                pltpu.VMEM((6, 68, 128), f32),
            ),
            in_specs=[pl.BlockSpec(memory_space=pltpu.HBM)] * 8,
            out_specs=(vmem, vmem, vmem),
            scratch_shapes=[
                pltpu.VMEM((19, 64, 128), f32),
                pltpu.VMEM((19, 8, 8, 128), bf16),
                pltpu.VMEM((8, 8, 128), jnp.int32),
                pltpu.VMEM((3, 16, 128), f32),
                pltpu.VMEM((3, 16, 128), f32),
                pltpu.VMEM((16, 128), jnp.int32),
                pltpu.SMEM((BLOCKS,), jnp.int32),
                pltpu.SMEM((BLOCKS,), jnp.int32),
                pltpu.VMEM((19, 64, 128), f32),
                pltpu.VMEM((19, 64, 128), f32),
                pltpu.VMEM((2, POST_TILES * 8, 128), f32),
                pltpu.VMEM((2, POST_TILES * 8, 128), f32),
                pltpu.VMEM((ROWS, 128), f32),
                pltpu.VMEM((24 * 8, 128), f32),
                pltpu.VMEM((72, 128), f32),
                pltpu.VMEM((2, 72, 128), f32),
                pltpu.VMEM((ROWS, 256), bf16),
                pltpu.VMEM((ROWS, 256), bf16),
                pltpu.VMEM((384, WIDE), bf16),
                pltpu.VMEM((12, 16, 128), f32),
                pltpu.VMEM((3, 16, 128), jnp.int32),
                pltpu.VMEM((BLOCKS, U_TILES * 8, 128), f32),
                pltpu.VMEM((PAIRS, 192, 256), f32),
                pltpu.VMEM((BLOCKS, 24, 128), f32),
                pltpu.VMEM((ROWS, WIDE), bf16),
                pltpu.VMEM((ROWS, WIDE), bf16),
                pltpu.VMEM((ROWS, 128), f32),
                pltpu.VMEM((ROWS, 128), f32),
                pltpu.VMEM((24 * 8, 128), f32),
                pltpu.VMEM((24 * 8, 128), f32),
                pltpu.VMEM((72, 128), f32),
                pltpu.VMEM((2, 72, 128), f32),
                pltpu.VMEM((BLOCKS * 8, 128), f32),
                pltpu.VMEM((416, 128), f32),
                pltpu.VMEM((416, 128), f32),
                pltpu.SemaphoreType.DMA((N_MSG,)),
                pltpu.SemaphoreType.DMA((N_MSG,)),
                pltpu.SemaphoreType.DMA((8,)),
            ],
            compiler_params=pltpu.CompilerParams(
                collective_id=0, has_side_effects=True, vmem_limit_bytes=36 * 1024 * 1024
            ),
            name="channel",
        )(
            *(
                pltpu.with_memory_space_constraint(x, pltpu.HBM)
                for x in (pops.reshape(19, 64, 128), coarse_pops, interface, drop_vel, drop_frac, home, counts, dest)
            )
        )
        state, force, arrived = pl.pallas_call(
            deliver,
            out_shape=(
                jax.ShapeDtypeStruct((19, 64, 128), f32),
                jax.ShapeDtypeStruct((3, 64, 128), f32),
                jax.ShapeDtypeStruct((6, 68, 128), f32),
            ),
            in_specs=[vmem] * 3,
            out_specs=(anywhere,) * 3,
            scratch_shapes=[pltpu.SemaphoreType.DMA((7,))],
            compiler_params=pltpu.CompilerParams(vmem_limit_bytes=8 * 1024 * 1024),
            name="deliver",
        )(*made)
        return state.reshape(19, 8, 8, 128), force.reshape(3, 8, 8, 128), arrived

    return jax.shard_map(
        local,
        mesh=mesh,
        in_specs=(
            P(None, "gz", "gy", "gx"),
            P(None, "gz", "gy", "gx"),
            P("gz", "gy", "gx"),
            P(None, ("gx", "gy", "gz"), None),
            P(None, ("gx", "gy", "gz"), None),
            P(("gx", "gy", "gz"), None),
            P(("gx", "gy", "gz")),
            P(("gx", "gy", "gz")),
        ),
        out_specs=(
            P(None, "gz", "gy", "gx"),
            P(None, "gz", "gy", "gx"),
            P(None, ("gx", "gy", "gz"), None),
        ),
        check_vma=False,
    )
```

```python
import math

import jax
import jax.numpy as jnp
import numpy as np
from jax import lax
from jax.experimental import pallas as pl
from jax.experimental.pallas import tpu as pltpu
from jax.sharding import PartitionSpec as P

lattice = [
    (0, 0, 0), (1, 0, 0), (-1, 0, 0), (0, 1, 0), (0, -1, 0), (0, 0, 1), (0, 0, -1),
    (1, 1, 0), (-1, -1, 0), (1, -1, 0), (-1, 1, 0), (1, 0, 1), (-1, 0, -1), (1, 0, -1),
    (-1, 0, 1), (0, 1, 1), (0, -1, -1), (0, 1, -1), (0, -1, 1),
]
weights_table = [1.0 / 3.0] + [1.0 / 18.0] * 6 + [1.0 / 36.0] * 12
opposite = [0, 2, 1, 4, 3, 6, 5, 8, 7, 10, 9, 12, 11, 14, 13, 16, 15, 18, 17]
inverse_tau = 0.8
relax = 0.5
couple = 8.0
f32 = jnp.float32
bf16 = jnp.bfloat16

face_pops = {}
for axis in range(3):
    for sign in (1, -1):
        d = [0, 0, 0]
        d[axis] = sign
        face_pops[tuple(d)] = [i for i in range(19) if lattice[i][axis] == sign]
post_msgs = {}
tiles = 0
for i in list(range(7, 19)) + [3, 4, 5, 6, 1, 2]:
    c = lattice[i]
    count = 1 if (abs(c[0]) + abs(c[1]) + abs(c[2]) > 1 or c[0] != 0) else 5
    post_msgs[c] = (tiles, count)
    tiles += count
POST_TILES = tiles

regions = {
    (0, 0): (0, 24),
    (-1, 0): (24, 6),
    (1, 0): (30, 3),
    (0, -1): (33, 6),
    (0, 1): (39, 3),
    (-1, -1): (42, 2),
    (1, -1): (44, 1),
    (-1, 1): (45, 1),
    (1, 1): (46, 1),
}
region_list = list(regions)[::-1]
ROWS = 48 * 8
all_dirs = [(x, y, z) for z in (-1, 0, 1) for y in (-1, 0, 1) for x in (-1, 0, 1) if (x, y, z) != (0, 0, 0)]
far_first = sorted(all_dirs, key=lambda d: -abs(d[0]) - abs(d[1]) - abs(d[2]))
near_dirs = [d for d in far_first if 0 in d]
U_TILES = 19
WIDE = 2048
N_POST = 18
N_MSG = 2 * N_POST + 3 * 26
PAIRS = 8
BLOCKS = 16
UNROLL = 4
GROUP = 12


def corner_rows(region):
    dy, dz = region
    ys = [7] if dy == 1 else [0, 1]
    zs = [7] if dz == 1 else [0, 1]
    return [(c, y, z) for c in range(3) for z in zs for y in ys]


def tile_rows(t):
    return pl.ds(t * 8, 8)


def kernel(
    sizes,
    pops_hbm, coarse_hbm, interface_hbm, drop_vel_hbm, drop_frac_hbm, home_hbm, counts_hbm, dest_hbm,
    state_out, force, arrived,
    pops, coarse, interface, drop_vel, drop_frac, home, counts, dest,
    posts, state_mid, psend, precv, vmain, vsend, pksend, pkrecv, va, vb, weights,
    taps, homes, spread_weights, tmain, partial, shi, slo, f_main, f_beyond, fsend, frecv, fpsend, fprecv, states, outbox, inbox,
    send_sem, recv_sem, in_sem,
):
    n_x, n_y, n_z = sizes
    me = (lax.axis_index("gx"), lax.axis_index("gy"), lax.axis_index("gz"))
    level = me[2]
    at_bottom = level == 0
    at_top = level == n_z - 1

    def moved_by(axis, step, size):
        if step == 0:
            return me[axis]
        return lax.rem(me[axis] + (step + size), size)

    coords = {
        (axis, step): moved_by(axis, step, size)
        for axis, size in enumerate(sizes)
        for step in (-1, 0, 1)
    }

    def device(d):
        return {"gx": coords[0, d[0]], "gy": coords[1, d[1]], "gz": coords[2, d[2]]}

    lane = lax.broadcasted_iota(jnp.int32, (8, 128), 1)
    sub = lax.broadcasted_iota(jnp.int32, (8, 128), 0)

    third = (lane * 171) >> 9
    outer_low = lane - third * 3 == 0
    started = []

    def copy(index, src, dst, d):
        made = pltpu.make_async_remote_copy(
            src_ref=src,
            dst_ref=dst,
            send_sem=send_sem.at[index],
            recv_sem=recv_sem.at[index],
            device_id=device(d),
            device_id_type=pl.DeviceIdType.MESH,
        )
        made.start()
        started.append(made)
        return made

    barrier = pltpu.get_barrier_semaphore()
    for d in near_dirs:
        pl.semaphore_signal(barrier, inc=1, device_id=device(d), device_id_type=pl.DeviceIdType.MESH)

    loads = []
    for n, (src, dst) in enumerate(
        (
            (pops_hbm, pops),
            (coarse_hbm, coarse),
            (interface_hbm, interface),
            (drop_vel_hbm, drop_vel),
            (drop_frac_hbm, drop_frac),
            (home_hbm, home),
            (counts_hbm, counts),
            (dest_hbm, dest),
        )
    ):
        loads.append(pltpu.make_async_copy(src, dst, in_sem.at[n]))
        loads[-1].start()
    def macroscopic(values):
        plus = {i: values[i] + values[i + 1] for i in range(1, 19, 2)}
        minus = {i: values[i] - values[i + 1] for i in range(1, 19, 2)}
        axes = plus[1] + plus[3] + plus[5]
        edges = (plus[7] + plus[9]) + (plus[11] + plus[13]) + (plus[15] + plus[17])
        density = values[0] * weights_table[0] + axes * weights_table[1] + edges * weights_table[7]
        inverse = 1.0 / density
        near, far = weights_table[1] * inverse, weights_table[7] * inverse
        flow = [
            minus[1] * near + ((minus[7] + minus[9]) + (minus[11] + minus[13])) * far,
            minus[3] * near + ((minus[7] - minus[9]) + (minus[15] + minus[17])) * far,
            minus[5] * near + ((minus[11] - minus[13]) + (minus[15] - minus[17])) * far,
        ]
        return density, flow

    def collide(source):
        @pl.loop(0, 8, unroll=2)
        def _(z):
            rows = pl.ds(pl.multiple_of(z * 8, 8), 8)
            values = [source[i, rows, :] for i in range(19)]
            density, flow = macroscopic(values)
            square = flow[0] * flow[0] + flow[1] * flow[1] + flow[2] * flow[2]
            inside = interface[z] == 1
            scaled = density * inverse_tau
            base = scaled - square * (1.5 * scaled)
            first, second = scaled * 3.0, scaled * 4.5

            def put(i, balance):
                relaxed = values[i] * (1.0 - inverse_tau) + balance
                posts[i, rows, :] = jnp.where(inside, coarse[i, z].astype(f32), relaxed)

            put(0, base)
            for i in range(1, 19, 2):
                along = None
                for axis in range(3):
                    sign = lattice[i][axis]
                    if sign == 1:
                        along = flow[axis] if along is None else along + flow[axis]
                    if sign == -1:
                        along = along - flow[axis]
                even = base + along * along * second
                odd = along * first
                put(i, even + odd)
                put(i + 1, even - odd)

    def pack_posts(r, part):
        for d, (first, count) in list(post_msgs.items())[part]:
            layer = {a: (7 if d[a] == 1 else 0) for a in (1, 2)}
            if d in face_pops:
                listed = face_pops[d]
            else:
                listed = [lattice.index(d)]
            if d[0] != 0 and d[1] == 0 and d[2] == 0:
                acc = jnp.zeros((8, 128), f32)
                from_lane = 127 if d[0] == 1 else 0
                for k, i in enumerate(listed):
                    for z in range(8):
                        spot = k * 8 + z
                        turned = pltpu.roll(posts[i, tile_rows(z), :], (spot - from_lane) % 128, 1)
                        acc = jnp.where(lane == spot, turned, acc)
                psend[r, tile_rows(first), :] = acc
            elif d[2] != 0:
                for k, i in enumerate(listed):
                    psend[r, tile_rows(first + k), :] = posts[i, tile_rows(layer[2]), :]
            else:
                for k, i in enumerate(listed):
                    psend[r, tile_rows(first + k), :] = posts[i, pl.ds(layer[1], 8, stride=8), :]

    edges, faces = slice(0, 12), slice(12, 18)

    def send_posts(r, part):
        for d, (first, count) in list(post_msgs.items())[part]:
            rows = pl.ds(first * 8, count * 8)
            post_copies[r].append(copy(len(started), psend.at[r, rows], precv.at[r, rows], d))

    post_copies = ([], [])

    def pull(r, i):
        cx, cy, cz = lattice[i]
        far = 127 if cx == 1 else 0

        def halo(d):
            first, count = post_msgs[d]
            k = face_pops[d].index(i) if d in face_pops and d[0] == 0 else 0
            return first + k

        def x_shift(value, beyond):
            return pltpu.roll(jnp.where(lane == far, beyond, value), cx % 128, 1)

        def y_shift(value, row):
            edge = 0 if cy == 1 else 7
            return jnp.where(sub == edge, row, pltpu.roll(value, cy % 8, 0))

        wanted = [z - cz for z in range(8)]
        planes = {z: posts[i, tile_rows(z), :] for z in range(8) if z in wanted}
        outer = None
        if cz != 0:
            outer = precv[r, tile_rows(halo((0, 0, cz))), :]
        if cx != 0:
            packed = precv[r, tile_rows(post_msgs[(cx, 0, 0)][0]), :]
            k = face_pops[(cx, 0, 0)].index(i)
            for z in planes:
                planes[z] = x_shift(planes[z], pltpu.roll(packed, (far - (k * 8 + z)) % 128, 1))
            if cz != 0:
                outer = x_shift(outer, precv[r, tile_rows(halo((cx, 0, cz))), :])
        if cy != 0:
            place = halo((0, cy, 0))
            if cx != 0:
                side = x_shift(precv[r, tile_rows(place), :], precv[r, tile_rows(halo((cx, cy, 0))), :])
                for z in planes:
                    planes[z] = y_shift(planes[z], side[z : z + 1, :])
            else:
                for z in planes:
                    planes[z] = y_shift(planes[z], precv[r, pl.ds(place * 8 + z, 1), :])
            if cz != 0:
                row = halo((0, cy, cz)) * 8 + (7 if cy == 1 else 0)
                outer = y_shift(outer, precv[r, pl.ds(row, 1), :])
        out = [planes[z] if z in planes else outer for z in wanted]
        if cz == 1:
            out[0] = jnp.where(at_bottom, posts[opposite[i], tile_rows(0), :], out[0])
        if cz == -1:
            out[7] = jnp.where(at_top, posts[opposite[i], tile_rows(7), :], out[7])
        return out

    def stream(r, copies, into):
        for made in copies:
            made.wait_recv()
        for i in range(19):
            out = pull(r, i)
            for z in range(8):
                into[i, tile_rows(z), :] = out[z]

    def prepare():
        for axis in range(3):
            angle = drop_frac[axis] * (0.5 * math.pi)
            sine = jnp.sin(angle)
            cosine = jnp.cos(angle)
            taps[axis * 4 + 0] = 0.25 - 0.25 * sine
            taps[axis * 4 + 1] = 0.25 + 0.25 * cosine
            taps[axis * 4 + 2] = 0.25 + 0.25 * sine
            taps[axis * 4 + 3] = 0.25 - 0.25 * cosine
        cells = home[...]
        homes[0] = (cells & 127) - 1
        homes[1] = ((cells >> 7) & 7) - 1
        homes[2] = (cells >> 10) - 1

    def picked(offset, weight):
        zero = jnp.zeros(offset.shape, f32)
        return jnp.where(
            offset == 0,
            weight[0],
            jnp.where(offset == 1, weight[1], jnp.where(offset == 2, weight[2], jnp.where(offset == 3, weight[3], zero))),
        )

    rows16 = lax.broadcasted_iota(jnp.int32, (16, 128), 0)

    def build_x_weights():
        @pl.loop(0, BLOCKS)
        def _(b):
            block = pl.ds(b, 1)
            lanes = pl.ds(pl.multiple_of(b * 128, 128), 128)
            first = homes[0, block, :]
            weight = [taps[k, block, :] for k in range(4)]
            for t in range(8):
                value = picked(rows16 + t * 16 - first, weight)
                high_part = value.astype(bf16)
                weights[pl.ds(t * 16, 16), lanes] = high_part
                weights[pl.ds(128 + t * 16, 16), lanes] = (value - high_part.astype(f32)).astype(bf16)
            def outside(at):
                row = rows16 - at
                cell = jnp.where(row == 0, -1, jnp.where(row == 1, 128, jnp.where(row == 2, 129, -1000)))
                return picked(cell - first, weight)

            value = outside(0)
            high_part = value.astype(bf16)
            weights[pl.ds(256, 16), lanes] = high_part
            weights[pl.ds(272, 16), lanes] = jnp.zeros((16, 128), bf16)
            weights[pl.ds(288, 16), lanes] = outside(8).astype(bf16)
            weights[pl.ds(304, 32), lanes] = jnp.zeros((32, 128), bf16)
            weights[pl.ds(336, 16), lanes] = (value - high_part.astype(f32)).astype(bf16)
            weights[pl.ds(352, 32), lanes] = jnp.zeros((32, 128), bf16)

    def build_yz_weights():
        @pl.loop(0, BLOCKS)
        def _(b):
            block = pl.ds(b, 1)
            hy = homes[1, block, :]
            hz = homes[2, block, :]
            wy = [taps[4 + k, block, :] for k in range(4)]
            wz = [taps[8 + k, block, :] for k in range(4)]
            y_main = picked(sub - hy, wy)
            z_main = picked(sub - hz, wz)
            y_out = [picked(y - hy, wy) for y in (8, 9, -1)]
            z_out = [picked(z - hz, wz) for z in (8, 9, -1)]
            z_out = [jnp.where(at_top, 0.0, z_out[0]), jnp.where(at_top, 0.0, z_out[1]), jnp.where(at_bottom, 0.0, z_out[2])]
            even = (sub & 1) == 0
            y_pair = jnp.where(even, y_out[0], y_out[1])
            z_pair = jnp.where(even, z_out[0], z_out[1])
            both = y_pair * jnp.where((sub & 2) == 0, z_out[0], z_out[1])
            made = [y_main * z_main[z : z + 1, :] for z in range(8)]
            made += [z_main * y_out[k] for k in range(3)]
            made += [y_main * z_out[k] for k in range(3)]
            made.append(both)
            made.append(jnp.where(sub < 4, both, 0.0))
            made.append(jnp.where(sub < 6, y_out[2] * z_pair, 0.0))
            made.append(jnp.where(sub < 6, y_pair * z_out[2], 0.0))
            made.append(jnp.where(sub < 3, y_out[2] * z_out[2], 0.0))
            for t in range(U_TILES):
                spread_weights[b, tile_rows(t), :] = made[t]

    for made in loads[:3]:
        made.wait()
    collide(pops)
    pack_posts(0, edges)
    pack_posts(0, faces)
    pl.semaphore_wait(barrier, len(near_dirs))
    send_posts(0, edges)
    send_posts(0, faces)
    stream(0, post_copies[0], state_mid)
    collide(state_mid)
    pack_posts(1, edges)
    send_posts(1, edges)
    pack_posts(1, faces)
    send_posts(1, faces)
    for made in loads[3:]:
        made.wait()
    prepare()
    build_x_weights()
    build_yz_weights()
    stream(1, post_copies[1], state_out)

    for z in range(8):
        values = [state_out[i, tile_rows(z), :] for i in range(19)]
        flow = macroscopic(values)[1]
        for c in range(3):
            vmain[tile_rows(c * 8 + z), :] = flow[c]

    def sent_tile(region, k):
        dy, dz = region
        if region == (0, 0):
            return vmain[tile_rows(k), :]
        if dz == 0:
            start = (k // 2) * 64 + k % 2 if dy == -1 else k * 64 + 7
            return vmain[pl.ds(start, 8, stride=8), :]
        if dy == 0:
            tile = (k // 2) * 8 + k % 2 if dz == -1 else k * 8 + 7
            return vmain[tile_rows(tile), :]
        acc = jnp.zeros((8, 128), f32)
        for r, (c, y, z) in enumerate(corner_rows(region)[k * 8 : k * 8 + 8]):
            acc = jnp.where(sub == r, vmain[pl.ds(c * 64 + z * 8 + y, 1), :], acc)
        return acc

    v_copies = {1: [], 2: [], 3: []}
    for n, region in enumerate(region_list):
        first, count = regions[region]
        packed = jnp.zeros((8, 128), f32)
        for k in range(count):
            value = sent_tile(region, k)
            if region != (0, 0):
                vsend[tile_rows(first - 24 + k), :] = value
            packed = jnp.where(third == k, pltpu.roll(value, 3 * k + 1, 1), packed)
        pksend[tile_rows(n), :] = packed
        for side, dx in ((0, -1), (1, 1)):
            part = pl.ds(n * 8, 8)
            made = copy(len(started), pksend.at[part], pkrecv.at[side, part], (dx,) + region)
            v_copies[1 + abs(region[0]) + abs(region[1])].append(made)
        if region != (0, 0):
            part = pl.ds((first - 24) * 8, count * 8)
            made = copy(len(started), vsend.at[part], vmain.at[pl.ds(first * 8, count * 8)], (0,) + region)
            v_copies[abs(region[0]) + abs(region[1])].append(made)

    def split_main(low, high):
        for t in range(low, high):
            rows = pl.ds(t * 16, 16)
            value = vmain[rows, :]
            high_part = value.astype(bf16)
            va[rows, pl.ds(0, 128)] = high_part
            vb[rows, pl.ds(0, 128)] = high_part
            va[rows, pl.ds(128, 128)] = (value - high_part.astype(f32)).astype(bf16)

    vmain[tile_rows(47), :] = jnp.zeros((8, 128), f32)
    split_main(0, 12)

    @pl.loop(0, PAIRS)
    def _(p):
        lanes = pl.ds(pl.multiple_of(p * 256, 256), 256)
        w_high = weights[pl.ds(0, 128), lanes]
        tmain[p] = jnp.dot(va[pl.ds(0, 192), :], jnp.concatenate([w_high, w_high], axis=0), preferred_element_type=f32)

    waited = 2 * N_POST
    for made in started[:waited]:
        made.wait_send()
    def unpack(n, region):
        first, count = regions[region]
        merged = jnp.where(outer_low, pkrecv[1, tile_rows(n), :], pkrecv[0, tile_rows(n), :])
        for g in range(0, count, GROUP):
            value = merged if g == 0 else pltpu.roll(merged, (-3 * g) % 128, 1)
            high_part = value.astype(bf16).astype(f32)
            low_part = pltpu.roll(value - high_part, 40, 1)
            value = jnp.where(lane < 40, high_part, jnp.where(lane < 80, low_part, pltpu.roll(high_part, 80, 1)))
            for k in range(g, min(g + GROUP, count)):
                beyond[first + k] = pltpu.roll(value, (-3 * (k - g)) % 128, 1) if k > g else value

    def store_beyond(low, high):
        for t in range(low, high):
            vb[pl.ds(t * 16, 16), pl.ds(128, 128)] = jnp.concatenate([beyond[2 * t], beyond[2 * t + 1]], axis=0).astype(bf16)

    beyond = {47: jnp.zeros((8, 128), f32)}
    for made in v_copies[1]:
        made.wait_recv()
    split_main(12, 21)
    unpack(region_list.index((0, 0)), (0, 0))
    store_beyond(0, 12)

    @pl.loop(0, PAIRS, unroll=UNROLL)
    def _(p):
        pair_lanes = pl.ds(pl.multiple_of(p * 256, 256), 256)
        w_high = weights[pl.ds(0, 128), pair_lanes]
        t_main = tmain[p] + jnp.dot(
            vb[pl.ds(0, 192), :], weights[pl.ds(128, 256), pair_lanes], preferred_element_type=f32
        )
        t_face = jnp.dot(
            va[pl.ds(192, 144), :], jnp.concatenate([w_high, w_high], axis=0), preferred_element_type=f32
        ) + jnp.dot(
            vb[pl.ds(192, 144), pl.ds(0, 128)], weights[pl.ds(128, 128), pair_lanes], preferred_element_type=f32
        )
        for j in range(2):
            b = 2 * p + j

            def tile(t):
                source, at = (t_main, t) if t < 24 else (t_face, t - 24)
                return source[at * 8 : at * 8 + 8, j * 128 : (j + 1) * 128]

            def u(t):
                return spread_weights[b, tile_rows(t), :]

            for c in range(3):
                acc = tile(24 + c * 2) * u(8) + tile(25 + c * 2) * u(9) + tile(30 + c) * u(10)
                acc = acc + tile(33 + c * 2) * u(11) + tile(34 + c * 2) * u(12) + tile(39 + c) * u(13)
                other = tile(c * 8) * u(0)
                for z in range(1, 8):
                    other = other + tile(c * 8 + z) * u(z)
                partial[b, tile_rows(c), :] = acc + other

    def corner_terms(tile, u):
        p42 = tile(42) * u(14)
        p43 = tile(43) * u(15)
        p445 = tile(44) * u(16) + tile(45) * u(17)
        p46 = tile(46) * u(18)
        terms = []
        for c in range(3):
            acc = jnp.where((sub >> 1) == c, p445, 0.0) + jnp.where(sub == c, p46, 0.0)
            terms.append(acc + (jnp.where((sub >> 2) == c, p42, 0.0) if c < 2 else p43))
        return terms

    for made in v_copies[2]:
        made.wait_recv()
    split_main(21, 24)
    for n, region in enumerate(region_list):
        if abs(region[0]) + abs(region[1]) == 1:
            unpack(n, region)
    store_beyond(12, 21)

    @pl.loop(0, PAIRS, unroll=UNROLL)
    def _(p):
        pair_lanes = pl.ds(pl.multiple_of(p * 256, 256), 256)
        w_high = weights[pl.ds(0, 128), pair_lanes]
        t_side = jnp.dot(
            vb[pl.ds(192, 144), pl.ds(128, 128)], weights[pl.ds(256, 128), pair_lanes], preferred_element_type=f32
        )
        t_corner = jnp.dot(
            va[pl.ds(336, 48), :], jnp.concatenate([w_high, w_high], axis=0), preferred_element_type=f32
        ) + jnp.dot(
            vb[pl.ds(336, 48), pl.ds(0, 128)], weights[pl.ds(128, 128), pair_lanes], preferred_element_type=f32
        )
        for j in range(2):
            b = 2 * p + j

            def tile(t):
                source, at = (t_side, t - 24) if t < 42 else (t_corner, t - 42)
                return source[at * 8 : at * 8 + 8, j * 128 : (j + 1) * 128]

            def u(t):
                return spread_weights[b, tile_rows(t), :]

            for c, acc in enumerate(corner_terms(tile, u)):
                acc = acc + tile(24 + c * 2) * u(8) + tile(25 + c * 2) * u(9) + tile(30 + c) * u(10)
                acc = acc + tile(33 + c * 2) * u(11) + tile(34 + c * 2) * u(12) + tile(39 + c) * u(13)
                partial[b, tile_rows(c), :] += acc

    for made in v_copies[3]:
        made.wait_recv()
    for n, region in enumerate(region_list):
        if abs(region[0]) + abs(region[1]) == 2:
            unpack(n, region)
    store_beyond(21, 24)

    @pl.loop(0, PAIRS, unroll=UNROLL)
    def _(p):
        pair_lanes = pl.ds(pl.multiple_of(p * 256, 256), 256)
        t_corner = jnp.dot(
            vb[pl.ds(336, 48), pl.ds(128, 128)], weights[pl.ds(256, 128), pair_lanes], preferred_element_type=f32
        )
        for j in range(2):
            b = 2 * p + j
            lanes = pl.ds(pl.multiple_of(p * 256 + j * 128, 128), 128)
            block = pl.ds(b, 1)

            def tile(t):
                return t_corner[(t - 42) * 8 : (t - 41) * 8, j * 128 : (j + 1) * 128]

            def u(t):
                return spread_weights[b, tile_rows(t), :]

            terms = corner_terms(tile, u)
            alive = lax.broadcasted_iota(jnp.int32, (1, 128), 1) < counts[b]
            pushes = []
            rows = []
            for c in range(3):
                acc = terms[c] + partial[b, tile_rows(c), :]
                sampled = jnp.sum(acc, axis=0, keepdims=True)
                speed = drop_vel[c, block, :]
                moved = speed + relax * (sampled - speed)
                pushes.append(jnp.where(alive, couple * (moved - sampled), 0.0))
                rows.append(jnp.where(alive, moved, 0.0))
            for c in range(3):
                rows.append(jnp.where(alive, drop_frac[c, block, :], 0.0) + rows[c])
            block_state = jnp.zeros((8, 128), f32)
            for c in range(6):
                block_state = jnp.where(sub == c, rows[c], block_state)
            states[pl.ds(pl.multiple_of(b * 8, 8), 8), :] = block_state

            by_half = jnp.where((sub >> 1) == 0, pushes[0], jnp.where((sub >> 1) == 1, pushes[1], pushes[2]))
            by_row = jnp.where(sub == 0, pushes[0], jnp.where(sub == 1, pushes[1], pushes[2]))
            by_four = jnp.where(sub < 4, pushes[0], pushes[1])
            plan = [(pushes[c], z) for c in range(3) for z in range(8)]
            plan += [(pushes[c], 8 + k) for c in range(3) for k in range(2)]
            plan += [(pushes[c], 10) for c in range(3)]
            plan += [(pushes[c], 11 + k) for c in range(3) for k in range(2)]
            plan += [(pushes[c], 13) for c in range(3)]
            plan += [(by_four, 14), (pushes[2], 15), (by_half, 16), (by_half, 17), (by_row, 18)]
            sources = [push * u(t) for push, t in plan] + [jnp.zeros((8, 128), f32)]
            for t in range(ROWS // 16):
                value = jnp.concatenate([sources[2 * t], sources[2 * t + 1]], axis=0)
                high_part = value.astype(bf16)
                shi[pl.ds(t * 16, 16), lanes] = high_part
                slo[pl.ds(t * 16, 16), lanes] = (value - high_part.astype(f32)).astype(bf16)

    codes = [dest[b] for b in range(BLOCKS)]
    wide = lax.broadcasted_iota(jnp.int32, (8, 128), 1)
    owner = wide >> 3
    code = jnp.zeros((8, 128), jnp.int32)
    for b in range(BLOCKS):
        code = jnp.where(owner == b, codes[b], code)
    rank = jnp.zeros((8, 128), jnp.int32)
    for b in range(BLOCKS):
        rank = rank + jnp.where((code == codes[b]) & (owner > b), 1, 0)
    lanes_of = jnp.where(code < 13, code, code - 1) * 2 + rank
    key = jnp.where(code == 13, -1, lanes_of * 8 + (wide & 7))[0:1, :]
    value = states[...]
    part_0 = value.astype(bf16)
    value = value - part_0.astype(f32)
    part_1 = value.astype(bf16)
    part_2 = (value - part_1.astype(f32)).astype(bf16)
    chosen = jnp.where(lax.broadcasted_iota(jnp.int32, (416, 128), 0) == key, 1.0, 0.0).astype(bf16)
    outbox[...] = (
        jnp.dot(chosen, part_0, preferred_element_type=f32)
        + jnp.dot(chosen, part_1, preferred_element_type=f32)
        + jnp.dot(chosen, part_2, preferred_element_type=f32)
    )
    h_copies = []

    def hand_over(hops):
        for d in far_first:
            if abs(d[0]) + abs(d[1]) + abs(d[2]) == hops:
                part = pl.ds(all_dirs.index(d) * 16, 16)
                h_copies.append(copy(len(started), outbox.at[part], inbox.at[part], d))

    hand_over(3)

    def over_droplets(source, weight):
        return lax.dot_general(source, weight, (((1,), (1,)), ((), ())), preferred_element_type=f32)

    shifted = lane - 80
    spot = jnp.where(lane < 36, third, jnp.where((lane >= 80) & (lane < 116), (shifted * 171) >> 9, -1))

    f_copies = []
    thirds = weights[pl.ds(256, 128), :]

    def spread_rows(low, count):
        rows = pl.ds(low, count)
        near = over_droplets(shi[rows, :], weights[pl.ds(0, 256), :])
        last = over_droplets(slo[rows, :], jnp.concatenate([weights[pl.ds(0, 128), :], thirds], axis=0))
        f_beyond[rows, :] = over_droplets(shi[rows, :], thirds) + last[:, 128:256]
        f_main[rows, :] = near[:, 0:128] + near[:, 128:256] + last[:, 0:128]

    spread_rows(192, 192)
    done = 2
    for n, region in enumerate(region_list):
        first, count = regions[region]
        if abs(region[0]) + abs(region[1]) < done:
            hand_over(done)
            done -= 1
            if done == 0:
                own = pl.ds(0, 192)
                f_beyond[own, :] = over_droplets(shi[own, :], thirds) + over_droplets(slo[own, :], thirds)
        packed = None
        for g in range(0, count, GROUP):
            value = jnp.zeros((8, 128), f32)
            for k in range(g, min(g + GROUP, count)):
                rows = tile_rows(first + k)
                if region != (0, 0):
                    fsend[tile_rows(first - 24 + k), :] = f_main[rows, :]
                both = f_beyond[rows, :]
                value = jnp.where(spot == k - g, pltpu.roll(both, 3 * (k - g), 1) if k > g else both, value)
            value = value + pltpu.roll(value, 48, 1)
            packed = value if g == 0 else jnp.where(lane < 3 * g, packed, pltpu.roll(value, 3 * g, 1))
        fpsend[tile_rows(n), :] = packed
        back = (-region[0], -region[1])
        for side, dx in ((0, -1), (1, 1)):
            part = pl.ds(n * 8, 8)
            f_copies.append(copy(len(started), fpsend.at[part], fprecv.at[side, part], (-dx,) + back))
        if region != (0, 0):
            part = pl.ds((first - 24) * 8, count * 8)
            f_copies.append(copy(len(started), fsend.at[part], frecv.at[part], (0,) + back))

    near = over_droplets(shi[own, :], weights[pl.ds(0, 256), :])
    last = over_droplets(slo[own, :], weights[pl.ds(0, 128), :])
    f_main[own, :] = near[:, 0:128] + near[:, 128:256] + last

    stay_rows = lax.broadcasted_iota(jnp.int32, (16, 128), 0)
    stays = jnp.zeros((16, 128), jnp.int32)
    for b in range(BLOCKS):
        stays = jnp.where(stay_rows == b, codes[b], stays)
    for c in range(6):
        arrived[c, pl.ds(0, 16), :] = jnp.where(stays == 13, states[pl.ds(c, 16, stride=8), :], 0.0)

    for made in started[waited : waited + 26]:
        made.wait_send()
    for made in f_copies:
        made.wait_recv()
    for n, region in enumerate(region_list):
        first, count = regions[region]
        merged = jnp.where(outer_low, fprecv[1, tile_rows(n), :], fprecv[0, tile_rows(n), :])
        for k in range(count):
            value = jnp.where((lane < 2) | (lane == 127), pltpu.roll(merged, (127 - 3 * k) % 128, 1), 0.0)
            rows = tile_rows(first + k)
            if region == (0, 0):
                f_main[rows, :] += value
            else:
                vmain[rows, :] = frecv[tile_rows(first - 24 + k), :] + value

    def row_of(t, r):
        return vmain[pl.ds(t * 8 + r, 1), :]

    def corner_row(region, c, y, z):
        return row_of(regions[region][0], corner_rows(region).index((c, y, z)))

    for c in range(3):
        for z in range(8):
            total = f_main[tile_rows(c * 8 + z), :]
            lines = [row_of(24 + c * 2, z), row_of(25 + c * 2, z), row_of(30 + c, z)]
            if z < 2 or z == 7:
                if z < 2:
                    total = total + vmain[tile_rows(33 + c * 2 + z), :]
                    low, high = (-1, -1), (1, -1)
                else:
                    total = total + vmain[tile_rows(39 + c), :]
                    low, high = (-1, 1), (1, 1)
                lines[0] = lines[0] + corner_row(low, c, 0, z)
                lines[1] = lines[1] + corner_row(low, c, 1, z)
                lines[2] = lines[2] + corner_row(high, c, 7, z)
            beside = jnp.where(sub == 0, lines[0], jnp.where(sub == 1, lines[1], jnp.where(sub == 7, lines[2], 0.0)))
            force[c, tile_rows(z), :] = total + beside

    for made in h_copies:
        made.wait_recv()
    for c in range(6):
        arrived[c, pl.ds(16, 52), :] = inbox[pl.ds(c, 52, stride=8), :]
    for made in started[waited + 26 :]:
        made.wait_send()


def deliver(state, force, arrived, state_hbm, force_hbm, arrived_hbm, sem):
    pairs = [(state.at[pl.ds(i, min(4, 19 - i))], state_hbm.at[pl.ds(i, min(4, 19 - i))]) for i in range(0, 19, 4)]
    pairs += [(arrived, arrived_hbm), (force, force_hbm)]
    copies = [pltpu.make_async_copy(src, dst, sem.at[n]) for n, (src, dst) in enumerate(pairs)]
    for made in copies:
        made.start()
    for made in copies:
        made.wait()


def solution(mesh):
    sizes = tuple(mesh.shape[a] for a in ("gx", "gy", "gz"))

    def body(*refs):
        kernel(sizes, *refs)

    def local(pops, coarse_pops, interface, drop_vel, drop_frac, home, counts, dest):
        vmem = pl.BlockSpec(memory_space=pltpu.VMEM)
        anywhere = pl.BlockSpec(memory_space=pl.ANY)
        made = pl.pallas_call(
            body,
            out_shape=(
                pltpu.VMEM((19, 64, 128), f32),
                pltpu.VMEM((3, 64, 128), f32),
                pltpu.VMEM((6, 68, 128), f32),
            ),
            in_specs=[pl.BlockSpec(memory_space=pltpu.HBM)] * 8,
            out_specs=(vmem, vmem, vmem),
            scratch_shapes=[
                pltpu.VMEM((19, 64, 128), f32),
                pltpu.VMEM((19, 8, 8, 128), bf16),
                pltpu.VMEM((8, 8, 128), jnp.int32),
                pltpu.VMEM((3, 16, 128), f32),
                pltpu.VMEM((3, 16, 128), f32),
                pltpu.VMEM((16, 128), jnp.int32),
                pltpu.SMEM((BLOCKS,), jnp.int32),
                pltpu.SMEM((BLOCKS,), jnp.int32),
                pltpu.VMEM((19, 64, 128), f32),
                pltpu.VMEM((19, 64, 128), f32),
                pltpu.VMEM((2, POST_TILES * 8, 128), f32),
                pltpu.VMEM((2, POST_TILES * 8, 128), f32),
                pltpu.VMEM((ROWS, 128), f32),
                pltpu.VMEM((24 * 8, 128), f32),
                pltpu.VMEM((72, 128), f32),
                pltpu.VMEM((2, 72, 128), f32),
                pltpu.VMEM((ROWS, 256), bf16),
                pltpu.VMEM((ROWS, 256), bf16),
                pltpu.VMEM((384, WIDE), bf16),
                pltpu.VMEM((12, 16, 128), f32),
                pltpu.VMEM((3, 16, 128), jnp.int32),
                pltpu.VMEM((BLOCKS, U_TILES * 8, 128), f32),
                pltpu.VMEM((PAIRS, 192, 256), f32),
                pltpu.VMEM((BLOCKS, 24, 128), f32),
                pltpu.VMEM((ROWS, WIDE), bf16),
                pltpu.VMEM((ROWS, WIDE), bf16),
                pltpu.VMEM((ROWS, 128), f32),
                pltpu.VMEM((ROWS, 128), f32),
                pltpu.VMEM((24 * 8, 128), f32),
                pltpu.VMEM((24 * 8, 128), f32),
                pltpu.VMEM((72, 128), f32),
                pltpu.VMEM((2, 72, 128), f32),
                pltpu.VMEM((BLOCKS * 8, 128), f32),
                pltpu.VMEM((416, 128), f32),
                pltpu.VMEM((416, 128), f32),
                pltpu.SemaphoreType.DMA((N_MSG,)),
                pltpu.SemaphoreType.DMA((N_MSG,)),
                pltpu.SemaphoreType.DMA((8,)),
            ],
            compiler_params=pltpu.CompilerParams(
                collective_id=0, has_side_effects=True, vmem_limit_bytes=36 * 1024 * 1024
            ),
            name="channel",
        )(
            *(
                pltpu.with_memory_space_constraint(x, pltpu.HBM)
                for x in (pops.reshape(19, 64, 128), coarse_pops, interface, drop_vel, drop_frac, home, counts, dest)
            )
        )
        state, force, arrived = pl.pallas_call(
            deliver,
            out_shape=(
                jax.ShapeDtypeStruct((19, 64, 128), f32),
                jax.ShapeDtypeStruct((3, 64, 128), f32),
                jax.ShapeDtypeStruct((6, 68, 128), f32),
            ),
            in_specs=[vmem] * 3,
            out_specs=(anywhere,) * 3,
            scratch_shapes=[pltpu.SemaphoreType.DMA((7,))],
            compiler_params=pltpu.CompilerParams(vmem_limit_bytes=8 * 1024 * 1024),
            name="deliver",
        )(*made)
        return state.reshape(19, 8, 8, 128), force.reshape(3, 8, 8, 128), arrived

    return jax.shard_map(
        local,
        mesh=mesh,
        in_specs=(
            P(None, "gz", "gy", "gx"),
            P(None, "gz", "gy", "gx"),
            P("gz", "gy", "gx"),
            P(None, ("gx", "gy", "gz"), None),
            P(None, ("gx", "gy", "gz"), None),
            P(("gx", "gy", "gz"), None),
            P(("gx", "gy", "gz")),
            P(("gx", "gy", "gz")),
        ),
        out_specs=(
            P(None, "gz", "gy", "gx"),
            P(None, "gz", "gy", "gx"),
            P(None, ("gx", "gy", "gz"), None),
        ),
        check_vma=False,
    )
```
